128 devices in a mesh: ax: 16 (over x, z_hi, core), xs: 8 (over z_lo, y).
Axes of the slice: x: 4, y: 4, z: 4 (z_hi: 2, z_lo: 2; z = z_hi * 2 + z_lo), core: 2. Of those that a mesh axis runs over, the one named last changes fastest.
Arguments:
- populations: float32 [19, 64, 512, 256], P(None, 'ax', 'xs'), may hold values from 0.001 to 0.75, as said below
- fluid_mask: int32 [64, 512, 256], P('ax', 'xs'), may hold values 0 or 1
- patch_voxel: int32 [1024, 512], P(('ax', 'xs')), may hold values from 0 to 65535
- patch_owner: int32 [1024], P(('ax', 'xs')), may hold values from 0 to 7, as said below
- positions: float32 [1024, 3, 512], P(('ax', 'xs')), may hold values from 0 to 5.5
- velocities: float32 [1024, 3, 512], P(('ax', 'xs')), may hold values from -6 to 6
- pair_tiles: int32 [1024, 8, 2], P(('ax', 'xs')), may hold values from 0 to 3
- pair_noise: bfloat16 [1024, 8, 128, 128], P(('ax', 'xs')), may hold values from -6 to 6
Outputs:
- populations_out: float32 [19, 64, 512, 256], P(None, 'ax', 'xs')
- new_positions: float32 [1024, 3, 512], P(('ax', 'xs'))
- new_velocities: float32 [1024, 3, 512], P(('ax', 'xs'))
- drag_field: float32 [3, 64, 512, 256], P(None, 'ax', 'xs')
The draws below stay inside these ranges and needn't reach their ends.
Inputs may be any that keep to these rules, and one draw needn't show every extreme that they name: `patch_owner`: among the 8 patches of every device, each index along xs is named exactly 1 times. `populations`: every distribution is positive.
All inputs are finite; a program needn't handle non-finite values. No bound on the sum of `fluid_mask` on one device may be relied on, other than what follows from the above.
Results may differ from the reference program's by a relative error of at most 0.0003.
Values sent between devices are 32-bit elements; how exact they have to be, the bound alone decides.
A program may use at most 128 MiB of HBM per device.

```python
import jax
import jax.numpy as jnp
from jax import lax

LX = 4
LY = 64
LZ = 256
PATCH_DEV = 8
NT = 4
PAIR_TILES = 8
TILE = 128
BEADS = 512
PER_OWNER = 1
NX = 64
NY = 512
PATCHES = 1024
N_XS = 8


LATTICE_DIRS = [(0, 0, 0), (1, 0, 0), (-1, 0, 0), (0, 1, 0), (0, -1, 0), (0, 0, 1), (0, 0, -1), (1, 1, 0), (-1, -1, 0), (1, -1, 0), (-1, 1, 0), (1, 0, 1), (-1, 0, -1), (1, 0, -1), (-1, 0, 1), (0, 1, 1), (0, -1, -1), (0, 1, -1), (0, -1, 1)]


LATTICE_WEIGHTS = [1.0 / 3.0] + [1.0 / 18.0] * 6 + [1.0 / 36.0] * 12


def draw_populations(key, part):
    key_one, key_two, key_three = jax.random.split(key, 3)
    cells = (NX, NY, LZ)
    density = jax.random.uniform(key_one, cells, jnp.float32, 0.85, 1.15)
    flow = jnp.clip(0.03 * jax.random.normal(key_two, (3,) + cells, jnp.float32), -0.08, 0.08)
    rough = jax.random.uniform(key_three, (19,) + cells, jnp.float32, 0.92, 1.08)
    out = []
    for index in range(19):
        dirx, diry, dirz = LATTICE_DIRS[index]
        proj = dirx * flow[0] + diry * flow[1] + dirz * flow[2]
        out.append(LATTICE_WEIGHTS[index] * density * (1.0 + 3.0 * proj) * rough[index])
    return jnp.stack(out).astype(jnp.float32)


def draw_patch_owner(key, part):
    blocks = PATCHES // PATCH_DEV
    keys = jax.random.split(key, blocks)
    perms = jax.vmap(lambda subkey: jax.random.permutation(subkey, PATCH_DEV))(keys)
    return (perms // PER_OWNER).reshape(PATCHES).astype(jnp.int32)


def place_ends(result, key, smallest, largest):
    extent = result.shape
    spot = [jax.random.randint(jax.random.fold_in(key, axis), (), 0, extent[axis]) for axis in range(len(extent))]
    result = result.at[tuple(spot)].set(smallest)
    longest = extent.index(max(extent))
    spot[longest] = (spot[longest] + 1) % extent[longest]
    return result.at[tuple(spot)].set(largest)


def steps_of(stream_key, shape, cuts, least, largest):
    level, own = 1.0, jax.random.fold_in(stream_key, 6)
    for dim, blocks in cuts:
        heights = jnp.exp(jax.random.uniform(jax.random.fold_in(own, dim), (blocks,), jnp.float32, least / len(cuts), largest / len(cuts)))
        level = level * jnp.repeat(heights, shape[dim] // blocks).reshape([-1 if axis == dim else 1 for axis in range(len(shape))])
    return level


def scatter_about(key, extent, scale, most, cuts=(), kind=jnp.bfloat16):
    result = scale * jax.random.normal(key, extent, jnp.float32)
    if cuts:
        result = result * steps_of(key, extent, cuts, -0.22, 0.18)
    return jnp.clip(result, -most, most).astype(kind)


def setup_inputs(seed: int = 0) -> dict:
    key_list = jax.random.split(jax.random.key(seed), 9)
    populations = draw_populations(jax.random.fold_in(key_list[8], 71), 0)
    fluid_mask = place_ends((jax.random.randint(key_list[1], (NX, NY, LZ), 0, 8) < 7).astype(jnp.int32), jax.random.fold_in(key_list[1], 1), 0, 1)
    patch_voxel = place_ends(jax.random.randint(key_list[2], (PATCHES, BEADS), 0, LX * LY * LZ), jax.random.fold_in(key_list[2], 1), 0, (LX * LY * LZ) - 1).astype(jnp.int32)
    patch_owner = draw_patch_owner(jax.random.fold_in(key_list[8], 71), 0)
    positions = jnp.clip(5.5 * jax.random.uniform(key_list[4], (PATCHES, 3, BEADS), jnp.float32) ** steps_of(key_list[4], (PATCHES, 3, BEADS), ((0, 128),), -0.2, 0.2), 0.0, 5.5)
    velocities = scatter_about(key_list[5], (PATCHES, 3, BEADS), 1.0, 6.0, ((0, 128),), jnp.float32)
    pair_tiles = place_ends(jax.random.randint(key_list[6], (PATCHES, PAIR_TILES, 2), 0, NT), jax.random.fold_in(key_list[6], 1), 0, NT - 1).astype(jnp.int32)
    pair_noise = scatter_about(key_list[7], (PATCHES, PAIR_TILES, TILE, TILE), 1.0, 6.0, ((0, 128),))
    return {"populations": populations, "fluid_mask": fluid_mask, "patch_voxel": patch_voxel, "patch_owner": patch_owner, "positions": positions, "velocities": velocities, "pair_tiles": pair_tiles, "pair_noise": pair_noise}


LATTICE_DIRS = [(0, 0, 0), (1, 0, 0), (-1, 0, 0), (0, 1, 0), (0, -1, 0), (0, 0, 1), (0, 0, -1), (1, 1, 0), (-1, -1, 0), (1, -1, 0), (-1, 1, 0), (1, 0, 1), (-1, 0, -1), (1, 0, -1), (-1, 0, 1), (0, 1, 1), (0, -1, -1), (0, 1, -1), (0, -1, 1)]
LATTICE_WEIGHTS = [1.0 / 3.0] + [1.0 / 18.0] * 6 + [1.0 / 36.0] * 12
OPPOSITE_DIR = [0, 2, 1, 4, 3, 6, 5, 8, 7, 10, 9, 12, 11, 14, 13, 16, 15, 18, 17]
RELAX_TIME = 0.8
TIME_STEP = 0.04
REPULSION = 25.0
FRICTION = 4.5
NOISE_AMP = 3.0
DRAG_COEFF = 12.5
VELOCITY_SCALE = 20.0
SOFTENING = 0.01

def moments(dist):
    density = lax.optimization_barrier(jnp.sum(dist, axis=0))
    comps = []
    for axis in range(3):
        total = jnp.zeros_like(density)
        for index in range(19):
            sign = LATTICE_DIRS[index][axis]
            if sign != 0:
                total = total + sign * dist[index]
        comps.append(total / density)
    return (density, comps)

def collide(dist):
    density, comps = moments(dist)
    speed_sq = comps[0] * comps[0] + comps[1] * comps[1] + comps[2] * comps[2]
    out = []
    for index in range(19):
        dirx, diry, dirz = LATTICE_DIRS[index]
        proj = dirx * comps[0] + diry * comps[1] + dirz * comps[2]
        equil = LATTICE_WEIGHTS[index] * density * (1.0 + 3.0 * proj + 4.5 * proj * proj - 1.5 * speed_sq)
        out.append(dist[index] - (dist[index] - equil) / RELAX_TIME)
    return jnp.stack(out)

def stream_padded(padded, post):
    size_x, size_y, size_z = (post.shape[1], post.shape[2], post.shape[3])
    out = []
    for index in range(19):
        dirx, diry, dirz = LATTICE_DIRS[index]
        start_x, start_y, start_z = (1 - dirx, 1 - diry, 1 - dirz)
        source = padded[index, start_x:start_x + size_x, start_y:start_y + size_y, start_z:start_z + size_z]
        source_mask = padded[19, start_x:start_x + size_x, start_y:start_y + size_y, start_z:start_z + size_z]
        out.append(jnp.where(source_mask > 0.5, source, post[OPPOSITE_DIR[index]]))
    return jnp.stack(out)

def lattice_step(dist, fluid):
    post = collide(dist)
    stacked = jnp.concatenate([post, fluid[None]], axis=0)
    wrapped = jnp.concatenate([stacked[:, -1:], stacked, stacked[:, :1]], axis=1)
    padded = jnp.pad(wrapped, ((0, 0), (0, 0), (1, 1), (1, 1)))
    return stream_padded(padded, post)

def pair_forces(position, velocity, pair_list, noise):
    tile = noise.shape[-1]
    count = position.shape[1] // tile
    pos_tiles = position.reshape(3, count, tile)
    vel_tiles = velocity.reshape(3, count, tile)

    def one_pair(carry, item):
        pair, noise_tile = item
        pos_a = lax.dynamic_index_in_dim(pos_tiles, pair[0], 1, keepdims=False)
        pos_b = lax.dynamic_index_in_dim(pos_tiles, pair[1], 1, keepdims=False)
        vel_a = lax.dynamic_index_in_dim(vel_tiles, pair[0], 1, keepdims=False)
        vel_b = lax.dynamic_index_in_dim(vel_tiles, pair[1], 1, keepdims=False)
        delta = pos_a[:, :, None] - pos_b[:, None, :]
        distance = jnp.sqrt(lax.optimization_barrier(jnp.sum(delta * delta, axis=0)) + SOFTENING)
        weight = jnp.maximum(0.0, 1.0 - distance)
        unit = delta / distance
        along = lax.optimization_barrier(jnp.sum(unit * (vel_a[:, :, None] - vel_b[:, None, :]), axis=0))
        scalar = REPULSION * weight - FRICTION * weight * weight * along + NOISE_AMP * weight * noise_tile.astype(jnp.float32) / jnp.sqrt(TIME_STEP)
        force = lax.optimization_barrier(jnp.sum(scalar[None] * unit, axis=2))
        current = lax.dynamic_index_in_dim(carry, pair[0], 1, keepdims=False)
        carry = lax.dynamic_update_index_in_dim(carry, current + force, pair[0], 1)
        return (carry, None)
    start = jnp.zeros((3, count, tile), jnp.float32)
    total, unused = lax.scan(one_pair, start, (pair_list, noise))
    return total.reshape(3, count * tile)

def patch_step(item):
    position, velocity, flow, pair_list, noise = item
    drag = DRAG_COEFF * (flow - velocity)
    new_vel = velocity + TIME_STEP * (pair_forces(position, velocity, pair_list, noise) + drag)
    new_pos = position + TIME_STEP * new_vel
    return (new_pos, new_vel, -TIME_STEP * drag)

def reference(populations, fluid_mask, patch_voxel, patch_owner, positions, velocities, pair_tiles, pair_noise):
    fluid = fluid_mask.astype(jnp.float32)
    dist = populations
    for step in range(2):
        dist = lattice_step(dist, fluid)
    density, comps = moments(dist)
    velocity_flat = VELOCITY_SCALE * jnp.stack(comps).reshape(3, NX * NY * LZ)
    blocks = PATCHES // PATCH_DEV
    owner_rows = patch_owner.reshape(blocks, PATCH_DEV)
    onehot = (owner_rows[:, :, None] == jnp.arange(N_XS, dtype=jnp.int32)[None, None, :]).astype(jnp.int32)
    rank = lax.optimization_barrier(jnp.sum(onehot * (jnp.cumsum(onehot, axis=1) - 1), axis=2))
    block_ids = jnp.arange(blocks, dtype=jnp.int32)[:, None]
    axial_idx = block_ids // N_XS
    cross_idx = block_ids % N_XS
    dest = ((axial_idx * N_XS + owner_rows) * PATCH_DEV + cross_idx * PER_OWNER + rank).reshape(PATCHES).astype(jnp.int32)
    row_block = (jnp.arange(PATCHES, dtype=jnp.int32) // PATCH_DEV)[:, None]
    local_x = patch_voxel // (LY * LZ)
    local_y = patch_voxel // LZ % LY
    local_z = patch_voxel % LZ
    global_id = ((row_block // N_XS * LX + local_x) * NY + row_block % N_XS * LY + local_y) * LZ + local_z
    global_id = global_id.astype(jnp.int32)
    at_source = jnp.transpose(velocity_flat[:, global_id], (1, 0, 2))
    owned = jnp.zeros_like(at_source).at[dest].set(at_source)
    new_pos, new_vel, reaction = lax.map(patch_step, (positions, velocities, owned, pair_tiles, pair_noise))
    back = reaction[dest]
    flat_ids = global_id.reshape(-1)
    field = jnp.stack([jax.ops.segment_sum(back[:, comp, :].reshape(-1), flat_ids, num_segments=NX * NY * LZ) for comp in range(3)])
    return (dist, new_pos, new_vel, field.reshape(3, NX, NY, LZ))
```

```python
import jax
import jax.numpy as jnp
from jax import lax
from jax.experimental import pallas as pl
from jax.experimental.pallas import tpu as pltpu
from jax.sharding import PartitionSpec as P

LATTICE_DIRS = [
    (0, 0, 0),
    (1, 0, 0),
    (-1, 0, 0),
    (0, 1, 0),
    (0, -1, 0),
    (0, 0, 1),
    (0, 0, -1),
    (1, 1, 0),
    (-1, -1, 0),
    (1, -1, 0),
    (-1, 1, 0),
    (1, 0, 1),
    (-1, 0, -1),
    (1, 0, -1),
    (-1, 0, 1),
    (0, 1, 1),
    (0, -1, -1),
    (0, 1, -1),
    (0, -1, 1),
]
LATTICE_WEIGHTS = [1.0 / 3.0] + [1.0 / 18.0] * 6 + [1.0 / 36.0] * 12
OPPOSITE_DIR = [0, 2, 1, 4, 3, 6, 5, 8, 7, 10, 9, 12, 11, 14, 13, 16, 15, 18, 17]
RELAX_TIME = 0.8
TIME_STEP = 0.04
REPULSION = 25.0
FRICTION = 4.5
NOISE_AMP = 3.0
NOISE_SCALE = 15.0
DRAG_COEFF = 12.5
VELOCITY_SCALE = 20.0
SOFTENING = 0.01
BF16 = jnp.bfloat16
F32 = jnp.float32


def padded_2(cells, sides, width, closed):
    for axis, dim in sides:
        count = lax.axis_size(axis)
        ends = count if closed else count - 1
        head = lax.slice_in_dim(cells, 0, width, axis=dim)
        tail = lax.slice_in_dim(cells, cells.shape[dim] - width, cells.shape[dim], axis=dim)
        cells = jnp.concatenate(
            [
                lax.ppermute(tail, axis, [(i, (i + 1) % count) for i in range(ends)]),
                cells,
                lax.ppermute(head, axis, [((i + 1) % count, i) for i in range(ends)]),
            ],
            axis=dim,
        )
    return cells


def moments(dist):
    density = jnp.sum(dist, axis=0)
    comps = []
    for axis in range(3):
        total = jnp.zeros_like(density)
        for index in range(19):
            sign = LATTICE_DIRS[index][axis]
            if sign != 0:
                total = total + sign * dist[index]
        comps.append(total / density)
    return (density, comps)


def collide(dist):
    density, comps = moments(dist)
    speed_sq = comps[0] * comps[0] + comps[1] * comps[1] + comps[2] * comps[2]
    out = []
    for index in range(19):
        dirx, diry, dirz = LATTICE_DIRS[index]
        proj = dirx * comps[0] + diry * comps[1] + dirz * comps[2]
        equil = (
            LATTICE_WEIGHTS[index]
            * density
            * (1.0 + 3.0 * proj + 4.5 * proj * proj - 1.5 * speed_sq)
        )
        out.append(dist[index] - (dist[index] - equil) / RELAX_TIME)
    return jnp.stack(out)


def stream_padded(padded, post):
    size_x, size_y, size_z = (post.shape[1], post.shape[2], post.shape[3])
    out = []
    for index in range(19):
        dirx, diry, dirz = LATTICE_DIRS[index]
        start_x, start_y, start_z = (1 - dirx, 1 - diry, 1 - dirz)
        source = padded[
            index,
            start_x : start_x + size_x,
            start_y : start_y + size_y,
            start_z : start_z + size_z,
        ]
        source_mask = padded[
            19, start_x : start_x + size_x, start_y : start_y + size_y, start_z : start_z + size_z
        ]
        out.append(jnp.where(source_mask > 0.5, source, post[OPPOSITE_DIR[index]]))
    return jnp.stack(out)


def pad_depth(block):
    return jnp.pad(block, ((0, 0), (0, 0), (0, 0), (1, 1)))


def lattice_step(dist, fluid):
    post = collide(dist)
    stacked = jnp.concatenate([post, fluid[None]], axis=0)
    axial = padded_2(stacked, (("ax", 1),), 1, True)
    full = padded_2(axial, (("xs", 2),), 1, False)
    return stream_padded(pad_depth(full), post)


def pair_patch(g, tiles, pos, vel, noise, force, rows, cols, noise_t):
    bead_tiles = rows.shape[0]
    pairs = noise.shape[1]
    tile = noise.shape[2]
    for t in range(bead_tiles):
        span = slice(t * tile, (t + 1) * tile)
        rows[t, 0:3, :] = pos[g, :, span]
        rows[t, 3:6, :] = vel[g, :, span]
        turned = rows[t].T
        for c in range(6):
            cols[t, c] = jnp.broadcast_to(turned[:, c : c + 1], (tile, tile))
    sub = lax.broadcasted_iota(jnp.int32, (tile, tile), 0)
    lane = lax.broadcasted_iota(jnp.int32, (tile, tile), 1)
    scaled_eye = jnp.where(sub == lane, NOISE_SCALE, 0.0).astype(BF16)
    step = 32

    def one_pair(p, carry):
        first, second = tiles[g, p, 0], tiles[g, p, 1]
        noise_t[...] = lax.dot_general(
            scaled_eye, noise[g, p], (((1,), (1,)), ((), ())), preferred_element_type=F32
        )
        own = rows[first]
        own = [jnp.broadcast_to(own[c : c + 1, :], (step, tile)) for c in range(6)]
        sums = [None] * 3
        for start in range(0, tile, step):
            part = slice(start, start + step)
            gap = [own[c] - cols[second, c, part, :] for c in range(6)]
            dist_sq = gap[0] * gap[0] + gap[1] * gap[1] + gap[2] * gap[2] + SOFTENING
            inverse = lax.rsqrt(dist_sq)
            weight = jnp.maximum(0.0, 1.0 - dist_sq * inverse)
            over = weight * inverse
            along = gap[0] * gap[3] + gap[1] * gap[4] + gap[2] * gap[5]
            scalar = over * (REPULSION + noise_t[part, :] - FRICTION * (over * along))
            for c in range(3):
                piece = (scalar * gap[c]).reshape(step // 8, 8, tile).sum(axis=0)
                sums[c] = piece if sums[c] is None else sums[c] + piece
        out = []
        for t in range(bead_tiles):
            for c in range(3):
                out.append(carry[t * 3 + c] + jnp.where(first == t, sums[c], 0.0))
        return tuple(out)

    zero = jnp.zeros((8, tile), F32)
    total = lax.fori_loop(0, pairs, one_pair, (zero,) * (3 * bead_tiles))
    for t in range(bead_tiles):
        for c in range(3):
            force[g, c : c + 1, t * tile : (t + 1) * tile] = total[t * 3 + c].sum(
                axis=0, keepdims=True
            )


def pair_kernel(tiles, pos, vel, noise, force, rows, cols, noise_t):
    lax.fori_loop(
        0,
        pos.shape[0],
        lambda g, _: (pair_patch(g, tiles, pos, vel, noise, force, rows, cols, noise_t), 0)[1],
        0,
    )


def pair_forces(pos, vel, tiles, noise):
    tile = noise.shape[2]
    count = pos.shape[2] // tile
    vmem = pl.BlockSpec(memory_space=pltpu.VMEM)
    return pl.pallas_call(
        pair_kernel,
        out_shape=jax.ShapeDtypeStruct(pos.shape, F32),
        in_specs=[pl.BlockSpec(memory_space=pltpu.SMEM), vmem, vmem, vmem],
        out_specs=vmem,
        scratch_shapes=[
            pltpu.VMEM((count, 8, tile), F32),
            pltpu.VMEM((count, 6, tile, tile), F32),
            pltpu.VMEM((tile, tile), F32),
        ],
        compiler_params=pltpu.CompilerParams(vmem_limit_bytes=32 * 2**20),
    )(tiles, pos, vel, noise)


def two_parts(value):
    high = value.astype(BF16)
    return high, (value - high.astype(F32)).astype(BF16)


def one_hot(index, size):
    beads = index.shape[1]
    rows = lax.broadcasted_iota(jnp.int32, (size, beads), 0)
    return jnp.where(rows == index, 1.0, 0.0).astype(BF16)


def gather_kernel(table, voxel, flow):
    depth = table.shape[2]
    lines = table.shape[1]
    parts = [two_parts(table[c]) for c in range(3)]

    def one_patch(g, _):
        index = voxel[pl.ds(g, 1), :]
        low, high = lax.rem(index, depth), lax.div(index, depth)
        hot = one_hot(low, depth)
        beads = index.shape[1]
        hit = lax.broadcasted_iota(jnp.int32, (lines, beads), 0) == high
        for c in range(3):
            got = jnp.dot(parts[c][0], hot, preferred_element_type=F32) + jnp.dot(
                parts[c][1], hot, preferred_element_type=F32
            )
            flow[g, c : c + 1, :] = VELOCITY_SCALE * jnp.where(hit, got, 0.0).sum(
                axis=0, keepdims=True
            )
        return 0

    lax.fori_loop(0, voxel.shape[0], one_patch, 0)


def scatter_kernel(reaction, voxel, field):
    lines, depth = field.shape[1], field.shape[2]
    field[...] = jnp.zeros_like(field)

    def one_patch(g, _):
        index = voxel[pl.ds(g, 1), :]
        low, high = lax.rem(index, depth), lax.div(index, depth)
        hot_low = one_hot(low, depth)
        hot_high = one_hot(high, lines)
        for c in range(3):
            line = jnp.broadcast_to(reaction[g, c : c + 1, :], (lines, index.shape[1]))
            total = field[c]
            for part in two_parts(line):
                total = total + lax.dot_general(
                    hot_high * part,
                    hot_low,
                    (((1,), (1,)), ((), ())),
                    preferred_element_type=F32,
                )
            field[c] = total
        return 0

    lax.fori_loop(0, voxel.shape[0], one_patch, 0)


def vmem_call(kernel, out_shape, *args):
    vmem = pl.BlockSpec(memory_space=pltpu.VMEM)
    return pl.pallas_call(
        kernel,
        out_shape=jax.ShapeDtypeStruct(out_shape, F32),
        in_specs=[vmem] * len(args),
        out_specs=vmem,
        compiler_params=pltpu.CompilerParams(vmem_limit_bytes=32 * 2**20),
    )(*args)


def per_device(
    populations, fluid_mask, patch_voxel, patch_owner, positions, velocities, pair_tiles, pair_noise
):
    fluid = fluid_mask.astype(jnp.float32)
    dist = populations
    for step in range(2):
        dist = lattice_step(dist, fluid)
    density, comps = moments(dist)
    size_x, size_y, size_z = dist.shape[1:]
    table = jnp.stack(comps).reshape(3, size_x * size_y, size_z)
    patch_count, bead_count = patch_voxel.shape
    owners = lax.axis_size("xs")
    share = patch_count // owners
    pair = pair_forces(positions, velocities, pair_tiles, pair_noise)
    at_beads = vmem_call(gather_kernel, (patch_count, 3, bead_count), table, patch_voxel)
    order = jnp.argsort(patch_owner, stable=True)
    grouped = at_beads[order].reshape(owners, share, 3, bead_count)
    received = lax.all_to_all(grouped, "xs", split_axis=0, concat_axis=0, tiled=True).reshape(
        patch_count, 3, bead_count
    )
    drag = DRAG_COEFF * (received - velocities)
    new_vel = velocities + TIME_STEP * (pair + drag)
    new_pos = positions + TIME_STEP * new_vel
    reaction = -TIME_STEP * drag
    returned = lax.all_to_all(
        reaction.reshape(owners, share, 3, bead_count),
        "xs",
        split_axis=0,
        concat_axis=0,
        tiled=True,
    )
    returned = returned.reshape(patch_count, 3, bead_count)
    back = returned[jnp.argsort(order)]
    field = vmem_call(scatter_kernel, (3, size_x * size_y, size_z), back, patch_voxel)
    return (dist, new_pos, new_vel, field.reshape(3, size_x, size_y, size_z))


def solution(mesh):
    return jax.shard_map(
        per_device,
        mesh=mesh,
        in_specs=(
            P(None, "ax", "xs", None),
            P("ax", "xs", None),
            P(("ax", "xs"), None),
            P(("ax", "xs")),
            P(("ax", "xs"), None, None),
            P(("ax", "xs"), None, None),
            P(("ax", "xs"), None, None),
            P(("ax", "xs"), None, None, None),
        ),
        out_specs=(
            P(None, "ax", "xs", None),
            P(("ax", "xs"), None, None),
            P(("ax", "xs"), None, None),
            P(None, "ax", "xs", None),
        ),
        check_vma=False,
    )
```

```python
import jax
import jax.numpy as jnp
from jax import lax
from jax.experimental import pallas as pl
from jax.experimental.pallas import tpu as pltpu
from jax.sharding import PartitionSpec as P

LATTICE_DIRS = [
    (0, 0, 0),
    (1, 0, 0),
    (-1, 0, 0),
    (0, 1, 0),
    (0, -1, 0),
    (0, 0, 1),
    (0, 0, -1),
    (1, 1, 0),
    (-1, -1, 0),
    (1, -1, 0),
    (-1, 1, 0),
    (1, 0, 1),
    (-1, 0, -1),
    (1, 0, -1),
    (-1, 0, 1),
    (0, 1, 1),
    (0, -1, -1),
    (0, 1, -1),
    (0, -1, 1),
]
LATTICE_WEIGHTS = [1.0 / 3.0] + [1.0 / 18.0] * 6 + [1.0 / 36.0] * 12
OPPOSITE_DIR = [0, 2, 1, 4, 3, 6, 5, 8, 7, 10, 9, 12, 11, 14, 13, 16, 15, 18, 17]
ORDER = [k for sign in (-1, 0, 1) for k in range(19) if LATTICE_DIRS[k][0] == sign]
SLOT = [ORDER.index(k) for k in range(19)]
PLUS_Y = [k for k in range(19) if LATTICE_DIRS[k][1] == 1]
MINUS_Y = [k for k in range(19) if LATTICE_DIRS[k][1] == -1]
CORNERS = [7, 8, 9, 10]
RELAX_TIME = 0.8
TIME_STEP = 0.04
REPULSION = 25.0
FRICTION = 4.5
NOISE_AMP = 3.0
NOISE_SCALE = 15.0
DRAG_COEFF = 12.5
VELOCITY_SCALE = 20.0
SOFTENING = 0.01
BF16 = jnp.bfloat16
F32 = jnp.float32
MESH = pl.DeviceIdType.MESH
PAD = 8


def moments(dist):
    density = dist[0]
    gaps = {}
    for k in range(1, 19, 2):
        density = density + (dist[k] + dist[k + 1])
        gaps[k] = dist[k] - dist[k + 1]
    inverse = 1.0 / density
    comps = []
    for axis in range(3):
        total = None
        for k in range(1, 19, 2):
            sign = LATTICE_DIRS[k][axis]
            if sign == 0:
                continue
            if total is None:
                total = gaps[k] if sign > 0 else -gaps[k]
            else:
                total = total + gaps[k] if sign > 0 else total - gaps[k]
        comps.append(total * inverse)
    return density, comps


def collide(dist):
    density, comps = moments(dist)
    base = 1.0 - 1.5 * (comps[0] * comps[0] + comps[1] * comps[1] + comps[2] * comps[2])
    gain = 1.0 / RELAX_TIME
    keep = 1.0 - gain
    out = [None] * 19
    out[0] = keep * dist[0] + (gain * LATTICE_WEIGHTS[0]) * density * base
    scaled = {w: (gain * w) * density for w in (1.0 / 18.0, 1.0 / 36.0)}
    for k in range(1, 19, 2):
        proj = None
        for axis in range(3):
            sign = LATTICE_DIRS[k][axis]
            if sign == 0:
                continue
            if proj is None:
                proj = comps[axis] if sign > 0 else -comps[axis]
            else:
                proj = proj + comps[axis] if sign > 0 else proj - comps[axis]
        amount = scaled[LATTICE_WEIGHTS[k]]
        even = amount * (base + 4.5 * (proj * proj))
        odd = amount * (3.0 * proj)
        out[k] = keep * dist[k] + (even + odd)
        out[k + 1] = keep * dist[k + 1] + (even - odd)
    return out


def shift_depth(value, amount):
    if amount == 0:
        return value
    return pltpu.roll(value, amount % value.shape[1], 1)


def block_rows(block):
    return pl.multiple_of(block * 8, 8)


def rows_behind(ref, lead, rows, amount):
    here = ref[(*lead, pl.ds(rows + PAD, 8), slice(None))]
    if amount == 0:
        return here
    sub = lax.broadcasted_iota(jnp.int32, here.shape, 0)
    beyond = ref[(*lead, pl.ds(rows + (PAD - 8 * amount), 8), slice(None))]
    mixed = jnp.where(sub == (7 if amount > 0 else 0), beyond, here)
    return pltpu.roll(mixed, amount % 8, 0)


def streamed(post, bits, plane, block):
    rows = block_rows(block)
    flags = bits[plane - 1, pl.ds(rows, 8), :]
    out = []
    for k in range(19):
        dirx, diry, dirz = LATTICE_DIRS[k]
        source = rows_behind(post, (plane - dirx, SLOT[k]), rows, diry)
        if k == 0:
            own = source
        else:
            own = post[plane, SLOT[OPPOSITE_DIR[k]], pl.ds(rows + PAD, 8), :]
        source = shift_depth(source, dirz)
        out.append(jnp.where((flags & (1 << k)) != 0, source, own))
    return out


def store_post(post, plane, block, values):
    for k in range(19):
        post[plane, SLOT[k], pl.ds(block_rows(block) + PAD, 8), :] = values[k]


def pair_patch(g, tiles, beads, noise, force, cols, noise_t):
    bead_tiles = beads.shape[1]
    pairs = noise.shape[1]
    tile = noise.shape[2]
    for t in range(bead_tiles):
        turned = beads[g, t].T
        for c in range(6):
            cols[t, c] = jnp.broadcast_to(turned[:, c : c + 1], (tile, tile))
    sub = lax.broadcasted_iota(jnp.int32, (tile, tile), 0)
    lane = lax.broadcasted_iota(jnp.int32, (tile, tile), 1)
    scaled_eye = jnp.where(sub == lane, NOISE_SCALE, 0.0).astype(BF16)
    step = 32

    def one_pair(p, carry):
        first, second = tiles[g, 0, p], tiles[g, 1, p]
        noise_t[...] = lax.dot_general(
            scaled_eye, noise[g, p], (((1,), (1,)), ((), ())), preferred_element_type=F32
        )
        own = beads[g, first]
        own = [jnp.broadcast_to(own[c : c + 1, :], (step, tile)) for c in range(6)]
        sums = [None] * 3
        for start in range(0, tile, step):
            part = slice(start, start + step)
            gap = [own[c] - cols[second, c, part, :] for c in range(6)]
            dist_sq = gap[0] * gap[0] + gap[1] * gap[1] + gap[2] * gap[2] + SOFTENING
            inverse = lax.rsqrt(dist_sq)
            weight = jnp.maximum(0.0, 1.0 - dist_sq * inverse)
            over = weight * inverse
            along = gap[0] * gap[3] + gap[1] * gap[4] + gap[2] * gap[5]
            scalar = over * (REPULSION + noise_t[part, :] - FRICTION * (over * along))
            for c in range(3):
                piece = (scalar * gap[c]).reshape(step // 8, 8, tile).sum(axis=0)
                sums[c] = piece if sums[c] is None else sums[c] + piece
        out = []
        for t in range(bead_tiles):
            for c in range(3):
                out.append(carry[t * 3 + c] + jnp.where(first == t, sums[c], 0.0))
        return tuple(out)

    zero = jnp.zeros((8, tile), F32)
    total = lax.fori_loop(0, pairs, one_pair, (zero,) * (3 * bead_tiles))
    for t in range(bead_tiles):
        for c in range(3):
            force[g, c : c + 1, t * tile : (t + 1) * tile] = total[t * 3 + c].sum(
                axis=0, keepdims=True
            )


def two_parts(value):
    high = value.astype(BF16)
    return high, (value - high.astype(F32)).astype(BF16)


def one_hot(index, size):
    beads = index.shape[1]
    rows = lax.broadcasted_iota(jnp.int32, (size, beads), 0)
    return jnp.where(rows == index, 1.0, 0.0).astype(BF16)


def repeat(count, body):
    lax.fori_loop(0, count, lambda i, _: (body(i), 0)[1], 0)


def step_kernel(
    n_ax,
    n_xs,
    tiles,
    owner,
    pops,
    mask,
    voxel,
    pos,
    vel,
    noise_hbm,
    pops_out,
    new_pos,
    new_vel,
    field,
    cells,
    post_a,
    post_b,
    flags,
    bits,
    noise,
    row_out,
    row_in,
    corner_out,
    corner_in,
    flag_row_out,
    flag_row_in,
    flag_corner_out,
    flag_corner_in,
    vel_in,
    flow,
    flow_out,
    flow_in,
    force,
    table,
    vel_out,
    tiled,
    cols,
    noise_t,
    load_sem,
    noise_sem,
    save_sem,
    near_send,
    near_recv,
    vel_send,
    vel_recv,
    flow_send,
    flow_recv,
):
    size_x, size_y, size_z = mask.shape
    blocks = size_y // 8
    top, bottom = PAD - 1, PAD + size_y
    first_row, last_row = PAD, PAD + size_y - 1
    own_rows = pl.ds(PAD, size_y)
    _, patches, beads = pos.shape
    me_ax, me_xs = lax.axis_index("ax"), lax.axis_index("xs")

    def at(move_ax, move_xs):
        return (lax.rem(me_ax + (move_ax + n_ax), n_ax), lax.rem(me_xs + (move_xs + n_xs), n_xs))

    loads = [
        pltpu.make_async_copy(pops.at[:, x], cells.at[:, x], load_sem.at[x]) for x in range(size_x)
    ]
    for x in (size_x - 1, 0, 1, 2):
        loads[x].start()
    noise_load = pltpu.make_async_copy(noise_hbm, noise, noise_sem)
    noise_load.start()

    partners = [at(1, 0), at(-1, 0)] + [at(0, d) for d in range(1, n_xs)]
    partners += [at(a, b) for a in (1, -1) for b in (1, -1)]
    barrier = pltpu.get_barrier_semaphore()
    for partner in partners:
        pl.semaphore_signal(barrier, inc=1, device_id=partner, device_id_type=MESH)

    tile = noise.shape[2]
    for g in range(patches):
        for c in range(3):
            vel_out[g, c : c + 1, :] = vel[c, g : g + 1, :]
            for t in range(beads // tile):
                span = slice(t * tile, (t + 1) * tile)
                tiled[g, t, c : c + 1, :] = pos[c, g : g + 1, span]
                tiled[g, t, c + 3 : c + 4, :] = vel[c, g : g + 1, span]

    for x in range(size_x):
        plane = mask[x].astype(F32)
        flags[x + 1, own_rows, :] = plane
        flag_row_out[0, x : x + 1, :] = plane[size_y - 1 : size_y, :]
        flag_row_out[1, x : x + 1, :] = plane[0:1, :]
    for c, k in enumerate(CORNERS):
        dirx, diry, _ = LATTICE_DIRS[k]
        x = size_x if dirx > 0 else 1
        y = last_row if diry > 0 else first_row
        flag_corner_out[c] = flags[x, y : y + 1, :]
    pl.semaphore_wait(barrier, len(partners))

    def exchange(part, faces, row_bufs, corner_bufs):
        targets = [at(1, 0), at(-1, 0), at(0, 1), at(0, -1)]
        targets += [at(LATTICE_DIRS[k][0], LATTICE_DIRS[k][1]) for k in CORNERS]
        ends = list(faces)
        ends += [(row_bufs[0].at[s], row_bufs[1].at[s]) for s in range(2)]
        ends += [(corner_bufs[0].at[c], corner_bufs[1].at[c]) for c in range(4)]
        return [
            pltpu.make_async_remote_copy(
                src_ref=src,
                dst_ref=dst,
                send_sem=near_send.at[part, i],
                recv_sem=near_recv.at[part, i],
                device_id=targets[i],
                device_id_type=MESH,
            )
            for i, (src, dst) in enumerate(ends)
        ]

    flag_copies = exchange(
        0,
        [
            (flags.at[size_x, own_rows], flags.at[0, own_rows]),
            (flags.at[1, own_rows], flags.at[size_x + 1, own_rows]),
        ],
        (flag_row_out, flag_row_in),
        (flag_corner_out, flag_corner_in),
    )
    for copy in flag_copies:
        copy.start()

    def to_group(source, target, send, recv):
        return [
            pltpu.make_async_remote_copy(
                src_ref=source.at[at(0, d)[1]],
                dst_ref=target.at[me_xs],
                send_sem=send.at[d - 1],
                recv_sem=recv.at[d - 1],
                device_id=at(0, d),
                device_id_type=MESH,
            )
            for d in range(1, n_xs)
        ]

    vel_copies = to_group(vel_out, vel_in, vel_send, vel_recv)
    for copy in vel_copies:
        copy.start()
    vel_in[me_xs] = vel_out[me_xs]

    def post_copies(part, post):
        return exchange(
            part,
            [
                (post.at[size_x, 14:19, own_rows], post.at[0, 14:19, own_rows]),
                (post.at[1, 0:5, own_rows], post.at[size_x + 1, 0:5, own_rows]),
            ],
            (row_out.at[part - 1], row_in.at[part - 1]),
            (corner_out.at[part - 1], corner_in.at[part - 1]),
        )

    def pack_rows(part, post):
        for i, k in enumerate(PLUS_Y):
            for x in range(size_x):
                row_out[part - 1, 0, i, x : x + 1, :] = post[
                    x + 1, SLOT[k], last_row : last_row + 1, :
                ]
        for i, k in enumerate(MINUS_Y):
            for x in range(size_x):
                row_out[part - 1, 1, i, x : x + 1, :] = post[
                    x + 1, SLOT[k], first_row : first_row + 1, :
                ]
        for c, k in enumerate(CORNERS):
            dirx, diry, _ = LATTICE_DIRS[k]
            x = size_x if dirx > 0 else 1
            y = last_row if diry > 0 else first_row
            corner_out[part - 1, c] = post[x, SLOT[k], y : y + 1, :]

    def unpack_rows(part, post):
        for i, k in enumerate(PLUS_Y):
            for x in range(size_x):
                post[x + 1, SLOT[k], top : top + 1, :] = row_in[part - 1, 0, i, x : x + 1, :]
        for i, k in enumerate(MINUS_Y):
            for x in range(size_x):
                post[x + 1, SLOT[k], bottom : bottom + 1, :] = row_in[part - 1, 1, i, x : x + 1, :]
        for c, k in enumerate(CORNERS):
            dirx, diry, _ = LATTICE_DIRS[k]
            x = 0 if dirx > 0 else size_x + 1
            y = top if diry > 0 else bottom
            post[x, SLOT[k], y : y + 1, :] = corner_in[part - 1, c]

    def collide_plane(x):
        def one_block(b):
            values = collide([cells[k, x, pl.ds(block_rows(b), 8), :] for k in range(19)])
            store_post(post_a, x + 1, b, values)

        repeat(blocks, one_block)

    copies_a = post_copies(1, post_a)
    loads[size_x - 1].wait()
    collide_plane(size_x - 1)
    copies_a[0].start()
    loads[0].wait()
    collide_plane(0)
    copies_a[1].start()
    for x in range(1, size_x - 1):
        loads[x].wait()
        collide_plane(x)
    pack_rows(1, post_a)
    for copy in copies_a[2:]:
        copy.start()

    for copy in flag_copies:
        copy.wait_recv()
    inside_low = me_xs > 0
    inside_high = me_xs < n_xs - 1
    for x in range(size_x):
        flags[x + 1, top : top + 1, :] = jnp.where(inside_low, flag_row_in[0, x : x + 1, :], 0.0)
        flags[x + 1, bottom : bottom + 1, :] = jnp.where(
            inside_high, flag_row_in[1, x : x + 1, :], 0.0
        )
    for c, k in enumerate(CORNERS):
        dirx, diry, _ = LATTICE_DIRS[k]
        x = 0 if dirx > 0 else size_x + 1
        y = top if diry > 0 else bottom
        flags[x, y : y + 1, :] = jnp.where(
            inside_low if diry > 0 else inside_high, flag_corner_in[c], 0.0
        )

    def bits_block(i):
        x, b = i // blocks, i % blocks
        here = block_rows(b)
        lane = lax.broadcasted_iota(jnp.int32, (8, size_z), 1)
        word = jnp.ones((8, size_z), jnp.int32)
        for k in range(1, 19):
            dirx, diry, dirz = LATTICE_DIRS[k]
            source = shift_depth(rows_behind(flags, (x + (1 - dirx),), here, diry), dirz)
            fluid = source > 0.5
            if dirz > 0:
                fluid = fluid & (lane > 0)
            elif dirz < 0:
                fluid = fluid & (lane < size_z - 1)
            word = word | jnp.where(fluid, 1 << k, 0)
        bits[x, pl.ds(here, 8), :] = word

    repeat(size_x * blocks, bits_block)

    def pair_range(start, stop):
        def one(g):
            pair_patch(start + g, tiles, tiled, noise, force, cols, noise_t)

        repeat(stop - start, one)

    noise_load.wait()
    half = patches // 2
    pair_range(0, half)

    for copy in copies_a:
        copy.wait_recv()
    unpack_rows(1, post_a)
    copies_b = post_copies(2, post_b)

    def advance_plane(plane):
        def one_block(b):
            store_post(post_b, plane, b, collide(streamed(post_a, bits, plane, b)))

        repeat(blocks, one_block)

    advance_plane(size_x)
    copies_b[0].start()
    advance_plane(1)
    copies_b[1].start()
    for plane in range(2, size_x):
        advance_plane(plane)
    pack_rows(2, post_b)
    for copy in copies_b[2:]:
        copy.start()

    pair_range(half, patches)

    for copy in copies_b:
        copy.wait_recv()
    unpack_rows(2, post_b)

    saves = [
        pltpu.make_async_copy(cells.at[:, x], pops_out.at[:, x], save_sem.at[x])
        for x in range(size_x)
    ]

    def finish_plane(plane):
        def one_block(b):
            values = streamed(post_b, bits, plane, b)
            here = block_rows(b)
            for k in range(19):
                cells[k, plane - 1, pl.ds(here, 8), :] = values[k]
            _, comps = moments(values)
            for c in range(3):
                table[c, pl.ds(here + (plane - 1) * size_y, 8), :] = comps[c]

        repeat(blocks, one_block)

    for plane in range(1, size_x + 1):
        finish_plane(plane)
        saves[plane - 1].start()

    lines = size_x * size_y

    def gather_patch(g):
        index = voxel[pl.ds(g, 1), :]
        low, high = lax.rem(index, size_z), lax.div(index, size_z)
        hot = one_hot(low, size_z)
        hit = lax.broadcasted_iota(jnp.int32, (lines, beads), 0) == high
        for c in range(3):
            parts = two_parts(table[c])
            got = jnp.dot(parts[0], hot, preferred_element_type=F32) + jnp.dot(
                parts[1], hot, preferred_element_type=F32
            )
            flow[g, c : c + 1, :] = VELOCITY_SCALE * jnp.where(hit, got, 0.0).sum(
                axis=0, keepdims=True
            )

    repeat(patches, gather_patch)
    for s in range(n_xs):
        row = jnp.int32(0)
        for g in range(patches):
            row = jnp.where(owner[g] == s, g, row)
        flow_out[s] = flow[row]
    flow_copies = to_group(flow_out, flow_in, flow_send, flow_recv)
    for copy in flow_copies:
        copy.start()
    flow_in[me_xs] = flow_out[me_xs]

    for copy in vel_copies:
        copy.wait_recv()
    field[...] = jnp.zeros_like(field)

    def scatter_patch(g):
        index = voxel[pl.ds(g, 1), :]
        low, high = lax.rem(index, size_z), lax.div(index, size_z)
        hot_low = one_hot(low, size_z)
        hot_high = one_hot(high, lines)
        reaction = -TIME_STEP * (DRAG_COEFF * (flow[g] - vel_in[owner[g]]))
        for c in range(3):
            line = jnp.broadcast_to(reaction[c : c + 1, :], (lines, beads))
            total = field[c]
            for part in two_parts(line):
                total = total + lax.dot_general(
                    hot_high * part,
                    hot_low,
                    (((1,), (1,)), ((), ())),
                    preferred_element_type=F32,
                )
            field[c] = total

    repeat(patches, scatter_patch)

    for copy in flow_copies:
        copy.wait_recv()
    for g in range(patches):
        drag = DRAG_COEFF * (flow_in[g] - vel_out[g])
        faster = vel_out[g] + TIME_STEP * (force[g] + drag)
        for c in range(3):
            new_vel[c, g : g + 1, :] = faster[c : c + 1, :]
    for c in range(3):
        new_pos[c] = pos[c] + TIME_STEP * new_vel[c]

    for copy in flag_copies + vel_copies + copies_a + copies_b + flow_copies:
        copy.wait_send()
    for copy in saves:
        copy.wait()


def per_device(
    n_ax, n_xs, populations, fluid_mask, patch_voxel, patch_owner, positions, velocities, pair_tiles, pair_noise
):
    size_x, size_y, size_z = fluid_mask.shape
    patches, _, beads = positions.shape
    tile = pair_noise.shape[2]
    count = beads // tile
    vmem = pl.BlockSpec(memory_space=pltpu.VMEM)
    smem = pl.BlockSpec(memory_space=pltpu.SMEM)
    hbm = pl.BlockSpec(memory_space=pl.ANY)
    high = size_y + 2 * PAD
    post = pltpu.VMEM((size_x + 2, 19, high, size_z), F32)
    beads3 = pltpu.VMEM((patches, 3, beads), F32)
    dma = pltpu.SemaphoreType.DMA

    def body(*refs):
        step_kernel(n_ax, n_xs, *refs)

    dist, new_pos, new_vel, field = pl.pallas_call(
        body,
        out_shape=(
            jax.ShapeDtypeStruct(populations.shape, F32),
            jax.ShapeDtypeStruct((3, patches, beads), F32),
            jax.ShapeDtypeStruct((3, patches, beads), F32),
            jax.ShapeDtypeStruct((3, size_x * size_y, size_z), F32),
        ),
        in_specs=[smem, smem, hbm, vmem, vmem, vmem, vmem, hbm],
        out_specs=(hbm, vmem, vmem, vmem),
        scratch_shapes=[
            pltpu.VMEM(populations.shape, F32),
            post,
            post,
            pltpu.VMEM((size_x + 2, high, size_z), F32),
            pltpu.VMEM((size_x, size_y, size_z), jnp.int32),
            pltpu.VMEM(pair_noise.shape, pair_noise.dtype),
            pltpu.VMEM((2, 2, 5, size_x, size_z), F32),
            pltpu.VMEM((2, 2, 5, size_x, size_z), F32),
            pltpu.VMEM((2, 4, 1, size_z), F32),
            pltpu.VMEM((2, 4, 1, size_z), F32),
            pltpu.VMEM((2, size_x, size_z), F32),
            pltpu.VMEM((2, size_x, size_z), F32),
            pltpu.VMEM((4, 1, size_z), F32),
            pltpu.VMEM((4, 1, size_z), F32),
            beads3,
            beads3,
            beads3,
            beads3,
            beads3,
            pltpu.VMEM((3, size_x * size_y, size_z), F32),
            beads3,
            pltpu.VMEM((patches, count, 8, tile), F32),
            pltpu.VMEM((count, 6, tile, tile), F32),
            pltpu.VMEM((tile, tile), F32),
            dma((size_x,)),
            dma,
            dma((size_x,)),
            dma((3, 8)),
            dma((3, 8)),
            dma((n_xs - 1,)),
            dma((n_xs - 1,)),
            dma((n_xs - 1,)),
            dma((n_xs - 1,)),
        ],
        compiler_params=pltpu.CompilerParams(
            collective_id=0, has_side_effects=True, vmem_limit_bytes=60 * 2**20
        ),
    )(
        jnp.transpose(pair_tiles, (0, 2, 1)),
        patch_owner,
        populations,
        fluid_mask,
        patch_voxel,
        jnp.transpose(positions, (1, 0, 2)),
        jnp.transpose(velocities, (1, 0, 2)),
        pair_noise,
    )
    new_pos, new_vel = (jnp.transpose(x, (1, 0, 2)) for x in (new_pos, new_vel))
    return (dist, new_pos, new_vel, field.reshape(3, size_x, size_y, size_z))


def solution(mesh):
    n_ax, n_xs = mesh.shape["ax"], mesh.shape["xs"]

    def step(*args):
        return per_device(n_ax, n_xs, *args)

    return jax.shard_map(
        step,
        mesh=mesh,
        in_specs=(
            P(None, "ax", "xs", None),
            P("ax", "xs", None),
            P(("ax", "xs"), None),
            P(("ax", "xs")),
            P(("ax", "xs"), None, None),
            P(("ax", "xs"), None, None),
            P(("ax", "xs"), None, None),
            P(("ax", "xs"), None, None, None),
        ),
        out_specs=(
            P(None, "ax", "xs", None),
            P(("ax", "xs"), None, None),
            P(("ax", "xs"), None, None),
            P(None, "ax", "xs", None),
        ),
        check_vma=False,
    )
```

```python
import jax
import jax.numpy as jnp
from jax import lax
from jax.experimental import pallas as pl
from jax.experimental.pallas import tpu as pltpu
from jax.sharding import PartitionSpec as P

LATTICE_DIRS = [
    (0, 0, 0),
    (1, 0, 0),
    (-1, 0, 0),
    (0, 1, 0),
    (0, -1, 0),
    (0, 0, 1),
    (0, 0, -1),
    (1, 1, 0),
    (-1, -1, 0),
    (1, -1, 0),
    (-1, 1, 0),
    (1, 0, 1),
    (-1, 0, -1),
    (1, 0, -1),
    (-1, 0, 1),
    (0, 1, 1),
    (0, -1, -1),
    (0, 1, -1),
    (0, -1, 1),
]
LATTICE_WEIGHTS = [1.0 / 3.0] + [1.0 / 18.0] * 6 + [1.0 / 36.0] * 12
OPPOSITE_DIR = [0, 2, 1, 4, 3, 6, 5, 8, 7, 10, 9, 12, 11, 14, 13, 16, 15, 18, 17]
ORDER = [k for sign in (-1, 0, 1) for k in range(19) if LATTICE_DIRS[k][0] == sign]
SLOT = [ORDER.index(k) for k in range(19)]
PLUS_Y = [k for k in range(19) if LATTICE_DIRS[k][1] == 1]
MINUS_Y = [k for k in range(19) if LATTICE_DIRS[k][1] == -1]
CORNERS = [7, 8, 9, 10]
RELAX_TIME = 0.8
TIME_STEP = 0.04
REPULSION = 25.0
FRICTION = 4.5
NOISE_AMP = 3.0
NOISE_SCALE = 15.0
DRAG_COEFF = 12.5
VELOCITY_SCALE = 20.0
SOFTENING = 0.01
BF16 = jnp.bfloat16
F32 = jnp.float32
MESH = pl.DeviceIdType.MESH
PAD = 8


def moments(dist):
    density = dist[0]
    gaps = {}
    for k in range(1, 19, 2):
        density = density + (dist[k] + dist[k + 1])
        gaps[k] = dist[k] - dist[k + 1]
    inverse = 1.0 / density
    comps = []
    for axis in range(3):
        total = None
        for k in range(1, 19, 2):
            sign = LATTICE_DIRS[k][axis]
            if sign == 0:
                continue
            if total is None:
                total = gaps[k] if sign > 0 else -gaps[k]
            else:
                total = total + gaps[k] if sign > 0 else total - gaps[k]
        comps.append(total * inverse)
    return density, comps


def collide(dist):
    density, comps = moments(dist)
    base = 1.0 - 1.5 * (comps[0] * comps[0] + comps[1] * comps[1] + comps[2] * comps[2])
    gain = 1.0 / RELAX_TIME
    keep = 1.0 - gain
    out = [None] * 19
    out[0] = keep * dist[0] + (gain * LATTICE_WEIGHTS[0]) * density * base
    scaled = {w: (gain * w) * density for w in (1.0 / 18.0, 1.0 / 36.0)}
    for k in range(1, 19, 2):
        proj = None
        for axis in range(3):
            sign = LATTICE_DIRS[k][axis]
            if sign == 0:
                continue
            if proj is None:
                proj = comps[axis] if sign > 0 else -comps[axis]
            else:
                proj = proj + comps[axis] if sign > 0 else proj - comps[axis]
        amount = scaled[LATTICE_WEIGHTS[k]]
        even = amount * (base + 4.5 * (proj * proj))
        odd = amount * (3.0 * proj)
        out[k] = keep * dist[k] + (even + odd)
        out[k + 1] = keep * dist[k + 1] + (even - odd)
    return out


def shift_depth(value, amount):
    if amount == 0:
        return value
    return pltpu.roll(value, amount % value.shape[1], 1)


def block_rows(block):
    return pl.multiple_of(block * 8, 8)


def rows_behind(ref, lead, rows, amount):
    here = ref[(*lead, pl.ds(rows + PAD, 8), slice(None))]
    if amount == 0:
        return here
    sub = lax.broadcasted_iota(jnp.int32, here.shape, 0)
    beyond = ref[(*lead, pl.ds(rows + (PAD - 8 * amount), 8), slice(None))]
    mixed = jnp.where(sub == (7 if amount > 0 else 0), beyond, here)
    return pltpu.roll(mixed, amount % 8, 0)


def streamed(post, bits, plane, block):
    rows = block_rows(block)
    flags = bits[plane - 1, pl.ds(rows, 8), :]
    out = []
    for k in range(19):
        dirx, diry, dirz = LATTICE_DIRS[k]
        source = rows_behind(post, (plane - dirx, SLOT[k]), rows, diry)
        if k == 0:
            own = source
        else:
            own = post[plane, SLOT[OPPOSITE_DIR[k]], pl.ds(rows + PAD, 8), :]
        source = shift_depth(source, dirz)
        out.append(jnp.where((flags & (1 << k)) != 0, source, own))
    return out


def store_post(post, plane, block, values):
    for k in range(19):
        post[plane, SLOT[k], pl.ds(block_rows(block) + PAD, 8), :] = values[k]


def pair_patch(g, tiles, beads, noise, force, cols, noise_t):
    bead_tiles = beads.shape[1]
    pairs = noise.shape[1]
    tile = noise.shape[2]
    sub = lax.broadcasted_iota(jnp.int32, (tile, tile), 0)
    lane = lax.broadcasted_iota(jnp.int32, (tile, tile), 1)
    scaled_eye = jnp.where(sub == lane, NOISE_SCALE, 0.0).astype(BF16)
    for p in range(pairs):
        noise_t[p] = lax.dot_general(
            scaled_eye, noise[g, p], (((1,), (1,)), ((), ())), preferred_element_type=F32
        )
    for t in range(bead_tiles):
        turned = beads[g, t].T
        for c in range(6):
            cols[t, c] = jnp.broadcast_to(turned[:, c : c + 1], (tile, tile))
    step = 32

    def one_pair(p, carry):
        first, second = tiles[g, 0, p], tiles[g, 1, p]
        own = beads[g, first]
        own = [jnp.broadcast_to(own[c : c + 1, :], (step, tile)) for c in range(6)]
        sums = [None] * 3
        for start in range(0, tile, step):
            part = slice(start, start + step)
            gap = [own[c] - cols[second, c, part, :] for c in range(6)]
            dist_sq = (gap[0] * gap[0] + gap[1] * gap[1]) + (gap[2] * gap[2] + SOFTENING)
            over = jnp.maximum(0.0, lax.rsqrt(dist_sq) - 1.0)
            along = gap[0] * gap[3] + gap[1] * gap[4] + gap[2] * gap[5]
            scalar = over * ((REPULSION + noise_t[p, part, :]) - over * along)
            for c in range(3):
                piece = (scalar * gap[c]).reshape(step // 8, 8, tile).sum(axis=0)
                sums[c] = piece if sums[c] is None else sums[c] + piece
        out = []
        for t in range(bead_tiles):
            for c in range(3):
                out.append(carry[t * 3 + c] + jnp.where(first == t, sums[c], 0.0))
        return tuple(out)

    def two_pairs(p, carry):
        return one_pair(2 * p + 1, one_pair(2 * p, carry))

    zero = jnp.zeros((8, tile), F32)
    total = lax.fori_loop(0, pairs // 2, two_pairs, (zero,) * (3 * bead_tiles))
    for t in range(bead_tiles):
        for c in range(3):
            force[g, c : c + 1, t * tile : (t + 1) * tile] = total[t * 3 + c].sum(
                axis=0, keepdims=True
            )


def two_parts(value):
    high = value.astype(BF16)
    return high, (value - high.astype(F32)).astype(BF16)


def one_hot(index, size):
    beads = index.shape[1]
    rows = lax.broadcasted_iota(jnp.int32, (size, beads), 0)
    return jnp.where(rows == index, 1.0, 0.0).astype(BF16)


def repeat(count, body):
    lax.fori_loop(0, count, lambda i, _: (body(i), 0)[1], 0)


def step_kernel(
    n_ax,
    n_xs,
    tiles_hbm,
    owner_hbm,
    pops,
    mask_hbm,
    voxel_hbm,
    pos_hbm,
    vel_hbm,
    noise_hbm,
    pops_out,
    new_pos,
    new_vel,
    field,
    tiles,
    owner,
    mask,
    voxel,
    pos,
    vel,
    hot_low,
    hot_high,
    parts,
    cells,
    post_a,
    post_b,
    flags,
    bits,
    noise,
    row_out_a,
    row_in_a,
    corner_out_a,
    corner_in_a,
    row_out_b,
    row_in_b,
    corner_out_b,
    corner_in_b,
    scaled,
    vel_in,
    flow,
    flow_out,
    flow_in,
    force,
    table,
    vel_out,
    tiled,
    cols,
    noise_t,
    load_sem,
    small_sem,
    save_sem,
    near_send,
    near_recv,
    vel_send,
    vel_recv,
    flow_send,
    flow_recv,
):
    size_x, size_y, size_z = mask_hbm.shape
    blocks = size_y // 8
    top, bottom = PAD - 1, PAD + size_y
    first_row, last_row = PAD, PAD + size_y - 1
    own_rows = pl.ds(PAD, size_y)
    _, patches, beads = pos_hbm.shape
    me_ax, me_xs = lax.axis_index("ax"), lax.axis_index("xs")

    def at(move_ax, move_xs):
        return (lax.rem(me_ax + (move_ax + n_ax), n_ax), lax.rem(me_xs + (move_xs + n_xs), n_xs))

    loads = [
        pltpu.make_async_copy(pops.at[:, x], cells.at[:, x], load_sem.at[x]) for x in range(size_x)
    ]
    smalls = [
        pltpu.make_async_copy(src, dst, small_sem.at[i])
        for i, (src, dst) in enumerate(
            [
                (mask_hbm, mask),
                (pos_hbm, pos),
                (vel_hbm, vel),
                (voxel_hbm, voxel),
                (tiles_hbm, tiles),
                (owner_hbm, owner),
                (noise_hbm, noise),
            ]
        )
    ]
    loads[size_x - 1].start()
    loads[0].start()
    for copy in smalls[:-1]:
        copy.start()
    for x in range(1, size_x - 1):
        loads[x].start()
    smalls[-1].start()

    partners = [at(1, 0), at(-1, 0)] + [at(0, d) for d in range(1, n_xs)]
    partners += [at(a, b) for a in (1, -1) for b in (1, -1)]
    barrier = pltpu.get_barrier_semaphore()
    for partner in partners:
        pl.semaphore_signal(barrier, inc=1, device_id=partner, device_id_type=MESH)

    def remote(src, dst, sems, spot, target):
        return pltpu.make_async_remote_copy(
            src_ref=src,
            dst_ref=dst,
            send_sem=sems[0].at[spot],
            recv_sem=sems[1].at[spot],
            device_id=target,
            device_id_type=MESH,
        )

    near = (near_send, near_recv)
    flag_copies = [
        remote(flags.at[size_x, own_rows], flags.at[0, own_rows], near, (0, 0), at(1, 0)),
        remote(flags.at[1, own_rows], flags.at[size_x + 1, own_rows], near, (0, 1), at(-1, 0)),
    ]

    def to_group(source, target, send, recv):
        return [
            pltpu.make_async_remote_copy(
                src_ref=source.at[at(0, d)[1]],
                dst_ref=target.at[me_xs],
                send_sem=send.at[d - 1],
                recv_sem=recv.at[d - 1],
                device_id=at(0, d),
                device_id_type=MESH,
            )
            for d in range(1, n_xs)
        ]

    def post_copies(part, post, row_bufs, corner_bufs):
        ends = [
            (post.at[size_x, 14:19, own_rows], post.at[0, 14:19, own_rows], at(1, 0)),
            (post.at[1, 0:5, own_rows], post.at[size_x + 1, 0:5, own_rows], at(-1, 0)),
        ]
        for side in range(2):
            ends.append((row_bufs[0].at[side], row_bufs[1].at[side], at(0, 1 - 2 * side)))
        for c, k in enumerate(CORNERS):
            target = at(LATTICE_DIRS[k][0], LATTICE_DIRS[k][1])
            ends.append((corner_bufs[0].at[c], corner_bufs[1].at[c], target))
        return [
            remote(src, dst, near, (part, i), target) for i, (src, dst, target) in enumerate(ends)
        ]

    def corner_spots(c, halo):
        dirx, diry, _ = LATTICE_DIRS[CORNERS[c]]
        if halo:
            return (0 if dirx > 0 else size_x + 1), (top if diry > 0 else bottom)
        return (size_x if dirx > 0 else 1), (last_row if diry > 0 else first_row)

    def pack_rows(post, row_buf, corner_buf):
        for side, dirs in enumerate((PLUS_Y, MINUS_Y)):
            y = first_row if side else last_row
            for i, k in enumerate(dirs):
                for x in range(size_x):
                    row_buf[side, i, x : x + 1, :] = post[x + 1, SLOT[k], y : y + 1, :]
        for c, k in enumerate(CORNERS):
            x, y = corner_spots(c, False)
            corner_buf[c, 0:1, :] = post[x, SLOT[k], y : y + 1, :]

    def unpack_rows(post, row_buf, corner_buf):
        for side, dirs in enumerate((PLUS_Y, MINUS_Y)):
            y = bottom if side else top
            for i, k in enumerate(dirs):
                for x in range(size_x):
                    post[x + 1, SLOT[k], y : y + 1, :] = row_buf[side, i, x : x + 1, :]
        for c, k in enumerate(CORNERS):
            x, y = corner_spots(c, True)
            post[x, SLOT[k], y : y + 1, :] = corner_buf[c, 0:1, :]

    def collide_plane(x):
        def one_block(b):
            values = collide([cells[k, x, pl.ds(block_rows(b), 8), :] for k in range(19)])
            store_post(post_a, x + 1, b, values)

        repeat(blocks, one_block)

    rows_a, corners_a = (row_out_a, row_in_a), (corner_out_a, corner_in_a)
    rows_b, corners_b = (row_out_b, row_in_b), (corner_out_b, corner_in_b)
    copies_a = post_copies(1, post_a, rows_a, corners_a)
    copies_b = post_copies(2, post_b, rows_b, corners_b)

    smalls[0].wait()
    for x in range(size_x):
        plane = mask[x].astype(F32)
        flags[x + 1, own_rows, :] = plane
        row_out_a[0, 5, x : x + 1, :] = plane[size_y - 1 : size_y, :]
        row_out_a[1, 5, x : x + 1, :] = plane[0:1, :]
    for c in range(4):
        x, y = corner_spots(c, False)
        corner_out_a[c, 1:2, :] = flags[x, y : y + 1, :]

    loads[size_x - 1].wait()
    collide_plane(size_x - 1)
    pl.semaphore_wait(barrier, len(partners))
    copies_a[0].start()
    loads[0].wait()
    collide_plane(0)
    copies_a[1].start()
    for copy in flag_copies:
        copy.start()
    for x in range(1, size_x - 1):
        loads[x].wait()
        collide_plane(x)
    pack_rows(post_a, row_out_a, corner_out_a)
    for copy in copies_a[2:]:
        copy.start()

    tile = noise.shape[2]
    smalls[1].wait()
    smalls[2].wait()
    for g in range(patches):
        for c in range(3):
            vel_out[g, c : c + 1, :] = vel[c, g : g + 1, :]
            for t in range(beads // tile):
                span = slice(t * tile, (t + 1) * tile)
                tiled[g, t, c : c + 1, :] = pos[c, g : g + 1, span]
                tiled[g, t, c + 3 : c + 4, :] = FRICTION * vel[c, g : g + 1, span]

    vel_copies = to_group(vel_out, vel_in, vel_send, vel_recv)
    for copy in vel_copies:
        copy.start()
    vel_in[me_xs] = vel_out[me_xs]

    def bits_block(i):
        x, b = i // blocks, i % blocks
        here = block_rows(b)
        lane = lax.broadcasted_iota(jnp.int32, (8, size_z), 1)
        word = jnp.ones((8, size_z), jnp.int32)
        for k in range(1, 19):
            dirx, diry, dirz = LATTICE_DIRS[k]
            source = shift_depth(rows_behind(flags, (x + (1 - dirx),), here, diry), dirz)
            fluid = source > 0.5
            if dirz > 0:
                fluid = fluid & (lane > 0)
            elif dirz < 0:
                fluid = fluid & (lane < size_z - 1)
            word = word | jnp.where(fluid, 1 << k, 0)
        bits[x, pl.ds(here, 8), :] = word

    def pair_range(start, stop):
        def one(g):
            pair_patch(start + g, tiles, tiled, noise, force, cols, noise_t)

        repeat(stop - start, one)

    lines = size_x * size_y
    smalls[3].wait()

    def hot_patch(g):
        index = voxel[pl.ds(g, 1), :]
        hot_low[g] = one_hot(lax.rem(index, size_z), size_z)
        hot_high[g] = one_hot(lax.div(index, size_z), lines)

    repeat(patches, hot_patch)

    for copy in smalls[4:]:
        copy.wait()
    early = patches // 2 - 1
    pair_range(0, early)

    for copy in flag_copies:
        copy.wait_recv()
    for copy in copies_a[2:]:
        copy.wait_recv()
    unpack_rows(post_a, row_in_a, corner_in_a)
    inside = (me_xs > 0, me_xs < n_xs - 1)
    for side in range(2):
        y = bottom if side else top
        for x in range(size_x):
            flags[x + 1, y : y + 1, :] = jnp.where(
                inside[side], row_in_a[side, 5, x : x + 1, :], 0.0
            )
    for c, k in enumerate(CORNERS):
        x, y = corner_spots(c, True)
        flags[x, y : y + 1, :] = jnp.where(
            inside[0 if LATTICE_DIRS[k][1] > 0 else 1], corner_in_a[c, 1:2, :], 0.0
        )
    repeat(size_x * blocks, bits_block)

    def advance_plane(plane):
        def one_block(b):
            store_post(post_b, plane, b, collide(streamed(post_a, bits, plane, b)))

        repeat(blocks, one_block)

    for plane in range(2, size_x):
        advance_plane(plane)
    copies_a[0].wait_recv()
    copies_a[1].wait_recv()
    advance_plane(size_x)
    copies_b[0].start()
    advance_plane(1)
    copies_b[1].start()
    pack_rows(post_b, row_out_b, corner_out_b)
    for copy in copies_b[2:]:
        copy.start()

    pair_range(early, patches)

    saves = [
        pltpu.make_async_copy(cells.at[:, x], pops_out.at[:, x], save_sem.at[x])
        for x in range(size_x)
    ]

    def finish_plane(plane):
        def one_block(b):
            values = streamed(post_b, bits, plane, b)
            here = block_rows(b)
            for k in range(19):
                cells[k, plane - 1, pl.ds(here, 8), :] = values[k]
            _, comps = moments(values)
            for c in range(3):
                table[plane - 1, c, pl.ds(here, 8), :] = comps[c]

        repeat(blocks, one_block)
        saves[plane - 1].start()

    def gather_planes(planes, first):
        low_line, high_line = planes[0] * size_y, planes[1] * size_y
        for n, plane in enumerate(planes):
            for c in range(3):
                spot = pl.ds((2 * c + n) * size_y, size_y)
                parts[0, spot, :], parts[1, spot, :] = two_parts(table[plane, c])

        def gather_patch(g):
            line = lax.div(voxel[pl.ds(g, 1), :], size_z)
            line = jnp.where(
                line >= high_line,
                jnp.where(line < high_line + size_y, line - (high_line - size_y), -1),
                jnp.where(line < low_line + size_y, line - low_line, -1),
            )
            hit = lax.broadcasted_iota(jnp.int32, (2 * size_y, beads), 0) == line
            got = jnp.dot(parts[0], hot_low[g], preferred_element_type=F32)
            got = got + jnp.dot(parts[1], hot_low[g], preferred_element_type=F32)
            for c in range(3):
                piece = got[2 * c * size_y : 2 * (c + 1) * size_y]
                piece = VELOCITY_SCALE * jnp.where(hit, piece, 0.0).sum(axis=0, keepdims=True)
                if first:
                    flow[g, c : c + 1, :] = piece
                else:
                    flow[g, c : c + 1, :] = flow[g, c : c + 1, :] + piece

        repeat(patches, gather_patch)

    for copy in copies_b[2:]:
        copy.wait_recv()
    unpack_rows(post_b, row_in_b, corner_in_b)
    finish_plane(2)
    finish_plane(3)
    gather_planes((1, 2), True)
    copies_b[0].wait_recv()
    copies_b[1].wait_recv()
    finish_plane(1)
    finish_plane(size_x)
    gather_planes((0, size_x - 1), False)
    for s in range(n_xs):
        row = jnp.int32(0)
        for g in range(patches):
            row = jnp.where(owner[g] == s, g, row)
        flow_out[s] = flow[row]
    flow_copies = to_group(flow_out, flow_in, flow_send, flow_recv)
    for copy in flow_copies:
        copy.start()
    flow_in[me_xs] = flow_out[me_xs]

    for copy in vel_copies:
        copy.wait_recv()
    def scatter_patch(g):
        reaction = -TIME_STEP * (DRAG_COEFF * (flow[g] - vel_in[owner[g]]))
        hot = hot_high[g].reshape(lines // 16, 16, beads)
        for c in range(3):
            line = jnp.broadcast_to(reaction[c : c + 1, :], (16, beads))
            for n, part in enumerate(two_parts(line)):
                scaled[n, c * lines : (c + 1) * lines, :] = (hot * part[None]).reshape(lines, beads)
        both = (((1,), (1,)), ((), ()))
        total = lax.dot_general(scaled[0], hot_low[g], both, preferred_element_type=F32)
        total = total + lax.dot_general(scaled[1], hot_low[g], both, preferred_element_type=F32)
        for c in range(3):
            field[c] = field[c] + total[c * lines : (c + 1) * lines]

    field[...] = jnp.zeros_like(field)
    repeat(patches, scatter_patch)

    for copy in flow_copies:
        copy.wait_recv()
    for g in range(patches):
        drag = DRAG_COEFF * (flow_in[g] - vel_out[g])
        faster = vel_out[g] + TIME_STEP * (force[g] + drag)
        for c in range(3):
            new_vel[c, g : g + 1, :] = faster[c : c + 1, :]
    for c in range(3):
        new_pos[c] = pos[c] + TIME_STEP * new_vel[c]

    for copy in flag_copies + vel_copies + copies_a + copies_b + flow_copies:
        copy.wait_send()
    for copy in saves:
        copy.wait()


def per_device(
    n_ax, n_xs, populations, fluid_mask, patch_voxel, patch_owner, positions, velocities, pair_tiles, pair_noise
):
    size_x, size_y, size_z = fluid_mask.shape
    patches, _, beads = positions.shape
    tile = pair_noise.shape[2]
    count = beads // tile
    vmem = pl.BlockSpec(memory_space=pltpu.VMEM)
    high = size_y + 2 * PAD
    post = pltpu.VMEM((size_x + 2, 19, high, size_z), F32)
    beads3 = pltpu.VMEM((patches, 3, beads), F32)
    dma = pltpu.SemaphoreType.DMA

    def body(*refs):
        step_kernel(n_ax, n_xs, *refs)

    dist, new_pos, new_vel, field = pl.pallas_call(
        body,
        out_shape=(
            jax.ShapeDtypeStruct(populations.shape, F32),
            jax.ShapeDtypeStruct((3, patches, beads), F32),
            jax.ShapeDtypeStruct((3, patches, beads), F32),
            jax.ShapeDtypeStruct((3, size_x * size_y, size_z), F32),
        ),
        in_specs=[pl.BlockSpec(memory_space=pltpu.HBM)] * 8,
        out_specs=(pl.BlockSpec(memory_space=pl.ANY), vmem, vmem, vmem),
        scratch_shapes=[
            pltpu.SMEM((patches, 2, pair_noise.shape[1]), jnp.int32),
            pltpu.SMEM((patches,), jnp.int32),
            pltpu.VMEM((size_x, size_y, size_z), jnp.int32),
            pltpu.VMEM((patches, beads), jnp.int32),
            pltpu.VMEM((3, patches, beads), F32),
            pltpu.VMEM((3, patches, beads), F32),
            pltpu.VMEM((patches, size_z, beads), BF16),
            pltpu.VMEM((patches, size_x * size_y, beads), BF16),
            pltpu.VMEM((2, 6 * size_y, size_z), BF16),
            pltpu.VMEM(populations.shape, F32),
            post,
            post,
            pltpu.VMEM((size_x + 2, high, size_z), F32),
            pltpu.VMEM((size_x, size_y, size_z), jnp.int32),
            pltpu.VMEM(pair_noise.shape, pair_noise.dtype),
            pltpu.VMEM((2, 6, size_x, size_z), F32),
            pltpu.VMEM((2, 6, size_x, size_z), F32),
            pltpu.VMEM((4, 2, size_z), F32),
            pltpu.VMEM((4, 2, size_z), F32),
            pltpu.VMEM((2, 5, size_x, size_z), F32),
            pltpu.VMEM((2, 5, size_x, size_z), F32),
            pltpu.VMEM((4, 1, size_z), F32),
            pltpu.VMEM((4, 1, size_z), F32),
            pltpu.VMEM((2, 3 * size_x * size_y, beads), BF16),
            beads3,
            beads3,
            beads3,
            beads3,
            beads3,
            pltpu.VMEM((size_x, 3, size_y, size_z), F32),
            beads3,
            pltpu.VMEM((patches, count, 8, tile), F32),
            pltpu.VMEM((count, 6, tile, tile), F32),
            pltpu.VMEM((pair_noise.shape[1], tile, tile), F32),
            dma((size_x,)),
            dma((7,)),
            dma((size_x,)),
            dma((3, 8)),
            dma((3, 8)),
            dma((n_xs - 1,)),
            dma((n_xs - 1,)),
            dma((n_xs - 1,)),
            dma((n_xs - 1,)),
        ],
        compiler_params=pltpu.CompilerParams(
            collective_id=0, has_side_effects=True, vmem_limit_bytes=44 * 2**20
        ),
    )(
        *(
            pltpu.with_memory_space_constraint(x, pltpu.HBM)
            for x in (
                jnp.transpose(pair_tiles, (0, 2, 1)),
                patch_owner,
                populations,
                fluid_mask,
                patch_voxel,
                jnp.transpose(positions, (1, 0, 2)),
                jnp.transpose(velocities, (1, 0, 2)),
                pair_noise,
            )
        )
    )
    new_pos, new_vel = (jnp.transpose(x, (1, 0, 2)) for x in (new_pos, new_vel))
    return (dist, new_pos, new_vel, field.reshape(3, size_x, size_y, size_z))


def solution(mesh):
    n_ax, n_xs = mesh.shape["ax"], mesh.shape["xs"]

    def step(*args):
        return per_device(n_ax, n_xs, *args)

    return jax.shard_map(
        step,
        mesh=mesh,
        in_specs=(
            P(None, "ax", "xs", None),
            P("ax", "xs", None),
            P(("ax", "xs"), None),
            P(("ax", "xs")),
            P(("ax", "xs"), None, None),
            P(("ax", "xs"), None, None),
            P(("ax", "xs"), None, None),
            P(("ax", "xs"), None, None, None),
        ),
        out_specs=(
            P(None, "ax", "xs", None),
            P(("ax", "xs"), None, None),
            P(("ax", "xs"), None, None),
            P(None, "ax", "xs", None),
        ),
        check_vma=False,
    )
```

```python
import jax
import jax.numpy as jnp
from jax import lax
from jax.experimental import pallas as pl
from jax.experimental.pallas import tpu as pltpu
from jax.sharding import PartitionSpec as P

LATTICE_DIRS = [
    (0, 0, 0),
    (1, 0, 0),
    (-1, 0, 0),
    (0, 1, 0),
    (0, -1, 0),
    (0, 0, 1),
    (0, 0, -1),
    (1, 1, 0),
    (-1, -1, 0),
    (1, -1, 0),
    (-1, 1, 0),
    (1, 0, 1),
    (-1, 0, -1),
    (1, 0, -1),
    (-1, 0, 1),
    (0, 1, 1),
    (0, -1, -1),
    (0, 1, -1),
    (0, -1, 1),
]
LATTICE_WEIGHTS = [1.0 / 3.0] + [1.0 / 18.0] * 6 + [1.0 / 36.0] * 12
OPPOSITE_DIR = [0, 2, 1, 4, 3, 6, 5, 8, 7, 10, 9, 12, 11, 14, 13, 16, 15, 18, 17]
ORDER = [k for sign in (-1, 0, 1) for k in range(19) if LATTICE_DIRS[k][0] == sign]
SLOT = [ORDER.index(k) for k in range(19)]
PLUS_Y = [k for k in range(19) if LATTICE_DIRS[k][1] == 1]
MINUS_Y = [k for k in range(19) if LATTICE_DIRS[k][1] == -1]
CORNERS = [7, 8, 9, 10]
RELAX_TIME = 0.8
TIME_STEP = 0.04
REPULSION = 25.0
FRICTION = 4.5
NOISE_AMP = 3.0
NOISE_SCALE = 15.0
DRAG_COEFF = 12.5
VELOCITY_SCALE = 20.0
SOFTENING = 0.01
BF16 = jnp.bfloat16
F32 = jnp.float32
MESH = pl.DeviceIdType.MESH
PAD = 8


def moments(dist):
    density = dist[0]
    gaps = {}
    for k in range(1, 19, 2):
        density = density + (dist[k] + dist[k + 1])
        gaps[k] = dist[k] - dist[k + 1]
    inverse = 1.0 / density
    comps = []
    for axis in range(3):
        total = None
        for k in range(1, 19, 2):
            sign = LATTICE_DIRS[k][axis]
            if sign == 0:
                continue
            if total is None:
                total = gaps[k] if sign > 0 else -gaps[k]
            else:
                total = total + gaps[k] if sign > 0 else total - gaps[k]
        comps.append(total * inverse)
    return density, comps


def collide(dist):
    density, comps = moments(dist)
    base = 1.0 - 1.5 * (comps[0] * comps[0] + comps[1] * comps[1] + comps[2] * comps[2])
    gain = 1.0 / RELAX_TIME
    keep = 1.0 - gain
    out = [None] * 19
    out[0] = keep * dist[0] + (gain * LATTICE_WEIGHTS[0]) * density * base
    scaled = {w: (gain * w) * density for w in (1.0 / 18.0, 1.0 / 36.0)}
    for k in range(1, 19, 2):
        proj = None
        for axis in range(3):
            sign = LATTICE_DIRS[k][axis]
            if sign == 0:
                continue
            if proj is None:
                proj = comps[axis] if sign > 0 else -comps[axis]
            else:
                proj = proj + comps[axis] if sign > 0 else proj - comps[axis]
        amount = scaled[LATTICE_WEIGHTS[k]]
        even = amount * (base + 4.5 * (proj * proj))
        odd = amount * (3.0 * proj)
        out[k] = keep * dist[k] + (even + odd)
        out[k + 1] = keep * dist[k + 1] + (even - odd)
    return out


def shift_depth(value, amount):
    if amount == 0:
        return value
    return pltpu.roll(value, amount % value.shape[1], 1)


def block_rows(block):
    return pl.multiple_of(block * 8, 8)


def rows_behind(ref, lead, rows, amount):
    here = ref[(*lead, pl.ds(rows + PAD, 8), slice(None))]
    if amount == 0:
        return here
    sub = lax.broadcasted_iota(jnp.int32, here.shape, 0)
    beyond = ref[(*lead, pl.ds(rows + (PAD - 8 * amount), 8), slice(None))]
    mixed = jnp.where(sub == (7 if amount > 0 else 0), beyond, here)
    return pltpu.roll(mixed, amount % 8, 0)


def streamed(post, bits, plane, block):
    rows = block_rows(block)
    flags = bits[plane - 1, pl.ds(rows, 8), :]
    out = []
    for k in range(19):
        dirx, diry, dirz = LATTICE_DIRS[k]
        source = rows_behind(post, (plane - dirx, SLOT[k]), rows, diry)
        if k == 0:
            own = source
        else:
            own = post[plane, SLOT[OPPOSITE_DIR[k]], pl.ds(rows + PAD, 8), :]
        source = shift_depth(source, dirz)
        out.append(jnp.where((flags & (1 << k)) != 0, source, own))
    return out


def store_post(post, plane, block, values):
    for k in range(19):
        post[plane, SLOT[k], pl.ds(block_rows(block) + PAD, 8), :] = values[k]


def pair_patch(g, tiles, beads, noise, force, cols, noise_t):
    bead_tiles = beads.shape[1]
    pairs = noise.shape[1]
    tile = noise.shape[2]
    sub = lax.broadcasted_iota(jnp.int32, (tile, tile), 0)
    lane = lax.broadcasted_iota(jnp.int32, (tile, tile), 1)
    scaled_eye = jnp.where(sub == lane, NOISE_SCALE, 0.0).astype(BF16)
    for p in range(pairs):
        noise_t[p] = lax.dot_general(
            scaled_eye, noise[g, p], (((1,), (1,)), ((), ())), preferred_element_type=F32
        )
    for t in range(bead_tiles):
        turned = beads[g, t].T
        for c in range(6):
            cols[t, c] = jnp.broadcast_to(turned[:, c : c + 1], (tile, tile))
    step = 32

    def one_pair(p, carry):
        first, second = tiles[g, 0, p], tiles[g, 1, p]
        own = beads[g, first]
        own = [jnp.broadcast_to(own[c : c + 1, :], (step, tile)) for c in range(6)]
        sums = [None] * 3
        for start in range(0, tile, step):
            part = slice(start, start + step)
            gap = [own[c] - cols[second, c, part, :] for c in range(6)]
            dist_sq = (gap[0] * gap[0] + gap[1] * gap[1]) + (gap[2] * gap[2] + SOFTENING)
            over = jnp.maximum(0.0, lax.rsqrt(dist_sq) - 1.0)
            along = gap[0] * gap[3] + gap[1] * gap[4] + gap[2] * gap[5]
            scalar = over * ((REPULSION + noise_t[p, part, :]) - over * along)
            for c in range(3):
                piece = (scalar * gap[c]).reshape(step // 8, 8, tile).sum(axis=0)
                sums[c] = piece if sums[c] is None else sums[c] + piece
        out = []
        for t in range(bead_tiles):
            for c in range(3):
                out.append(carry[t * 3 + c] + jnp.where(first == t, sums[c], 0.0))
        return tuple(out)

    def two_pairs(p, carry):
        return one_pair(2 * p + 1, one_pair(2 * p, carry))

    zero = jnp.zeros((8, tile), F32)
    total = lax.fori_loop(0, pairs // 2, two_pairs, (zero,) * (3 * bead_tiles))
    for t in range(bead_tiles):
        for c in range(3):
            force[g, c : c + 1, t * tile : (t + 1) * tile] = total[t * 3 + c].sum(
                axis=0, keepdims=True
            )


def two_parts(value):
    high = value.astype(BF16)
    return high, (value - high.astype(F32)).astype(BF16)


def one_hot(index, size):
    beads = index.shape[1]
    rows = lax.broadcasted_iota(jnp.int32, (size, beads), 0)
    return jnp.where(rows == index, 1.0, 0.0).astype(BF16)


def repeat(count, body, together=1):
    def turn(i, carry):
        for n in range(together):
            body(i * together + n)
        return carry

    lax.fori_loop(0, count // together, turn, 0)


def step_kernel(
    n_ax,
    n_xs,
    tiles_hbm,
    owner_hbm,
    pops,
    mask_hbm,
    voxel_hbm,
    pos_hbm,
    vel_hbm,
    noise_hbm,
    pops_out,
    new_pos,
    new_vel,
    field,
    tiles,
    owner,
    mask,
    voxel,
    pos,
    vel,
    hot_low,
    hot_high,
    parts,
    cells,
    post_a,
    post_b,
    flags,
    bits,
    noise,
    row_out_a,
    row_in_a,
    corner_out_a,
    corner_in_a,
    row_out_b,
    row_in_b,
    corner_out_b,
    corner_in_b,
    scaled,
    vel_in,
    flow,
    flow_out,
    flow_in,
    force,
    table,
    vel_out,
    tiled,
    cols,
    noise_t,
    load_sem,
    small_sem,
    save_sem,
    near_send,
    near_recv,
    vel_send,
    vel_recv,
    flow_send,
    flow_recv,
):
    size_x, size_y, size_z = mask_hbm.shape
    blocks = size_y // 8
    top, bottom = PAD - 1, PAD + size_y
    first_row, last_row = PAD, PAD + size_y - 1
    own_rows = pl.ds(PAD, size_y)
    _, patches, beads = pos_hbm.shape
    me_ax, me_xs = lax.axis_index("ax"), lax.axis_index("xs")

    def at(move_ax, move_xs):
        return (lax.rem(me_ax + (move_ax + n_ax), n_ax), lax.rem(me_xs + (move_xs + n_xs), n_xs))

    loads = [
        pltpu.make_async_copy(pops.at[:, x], cells.at[:, x], load_sem.at[x]) for x in range(size_x)
    ]
    smalls = [
        pltpu.make_async_copy(src, dst, small_sem.at[i])
        for i, (src, dst) in enumerate(
            [
                (mask_hbm, mask),
                (pos_hbm, pos),
                (vel_hbm, vel),
                (voxel_hbm, voxel),
                (tiles_hbm, tiles),
                (owner_hbm, owner),
                (noise_hbm, noise),
            ]
        )
    ]
    loads[size_x - 1].start()
    loads[0].start()
    for copy in smalls[:-1]:
        copy.start()
    for x in range(1, size_x - 1):
        loads[x].start()
    smalls[-1].start()

    partners = [at(1, 0), at(-1, 0)] + [at(0, d) for d in range(1, n_xs)]
    partners += [at(a, b) for a in (1, -1) for b in (1, -1)]
    barrier = pltpu.get_barrier_semaphore()
    for partner in partners:
        pl.semaphore_signal(barrier, inc=1, device_id=partner, device_id_type=MESH)

    def remote(src, dst, sems, spot, target):
        return pltpu.make_async_remote_copy(
            src_ref=src,
            dst_ref=dst,
            send_sem=sems[0].at[spot],
            recv_sem=sems[1].at[spot],
            device_id=target,
            device_id_type=MESH,
        )

    near = (near_send, near_recv)
    flag_copies = [
        remote(flags.at[size_x, own_rows], flags.at[0, own_rows], near, (0, 0), at(1, 0)),
        remote(flags.at[1, own_rows], flags.at[size_x + 1, own_rows], near, (0, 1), at(-1, 0)),
    ]

    def to_group(source, target, send, recv):
        return [
            pltpu.make_async_remote_copy(
                src_ref=source.at[at(0, d)[1]],
                dst_ref=target.at[me_xs],
                send_sem=send.at[d - 1],
                recv_sem=recv.at[d - 1],
                device_id=at(0, d),
                device_id_type=MESH,
            )
            for d in range(1, n_xs)
        ]

    def post_copies(part, post, row_bufs, corner_bufs):
        ends = [
            (post.at[size_x, 14:19, own_rows], post.at[0, 14:19, own_rows], at(1, 0)),
            (post.at[1, 0:5, own_rows], post.at[size_x + 1, 0:5, own_rows], at(-1, 0)),
        ]
        for side in range(2):
            ends.append((row_bufs[0].at[side], row_bufs[1].at[side], at(0, 1 - 2 * side)))
        for c, k in enumerate(CORNERS):
            target = at(LATTICE_DIRS[k][0], LATTICE_DIRS[k][1])
            ends.append((corner_bufs[0].at[c], corner_bufs[1].at[c], target))
        return [
            remote(src, dst, near, (part, i), target) for i, (src, dst, target) in enumerate(ends)
        ]

    def corner_spots(c, halo):
        dirx, diry, _ = LATTICE_DIRS[CORNERS[c]]
        if halo:
            return (0 if dirx > 0 else size_x + 1), (top if diry > 0 else bottom)
        return (size_x if dirx > 0 else 1), (last_row if diry > 0 else first_row)

    def pack_rows(post, row_buf, corner_buf):
        for side, dirs in enumerate((PLUS_Y, MINUS_Y)):
            y = first_row if side else last_row
            for i, k in enumerate(dirs):
                for x in range(size_x):
                    row_buf[side, i, x : x + 1, :] = post[x + 1, SLOT[k], y : y + 1, :]
        for c, k in enumerate(CORNERS):
            x, y = corner_spots(c, False)
            corner_buf[c, 0:1, :] = post[x, SLOT[k], y : y + 1, :]

    def unpack_rows(post, row_buf, corner_buf):
        for side, dirs in enumerate((PLUS_Y, MINUS_Y)):
            y = bottom if side else top
            for i, k in enumerate(dirs):
                for x in range(size_x):
                    post[x + 1, SLOT[k], y : y + 1, :] = row_buf[side, i, x : x + 1, :]
        for c, k in enumerate(CORNERS):
            x, y = corner_spots(c, True)
            post[x, SLOT[k], y : y + 1, :] = corner_buf[c, 0:1, :]

    def collide_plane(x):
        def one_block(b):
            values = collide([cells[k, x, pl.ds(block_rows(b), 8), :] for k in range(19)])
            store_post(post_a, x + 1, b, values)

        repeat(blocks, one_block, 8)

    rows_a, corners_a = (row_out_a, row_in_a), (corner_out_a, corner_in_a)
    rows_b, corners_b = (row_out_b, row_in_b), (corner_out_b, corner_in_b)
    copies_a = post_copies(1, post_a, rows_a, corners_a)
    copies_b = post_copies(2, post_b, rows_b, corners_b)

    smalls[0].wait()
    for x in range(size_x):
        plane = mask[x].astype(F32)
        flags[x + 1, own_rows, :] = plane
        row_out_a[0, 5, x : x + 1, :] = plane[size_y - 1 : size_y, :]
        row_out_a[1, 5, x : x + 1, :] = plane[0:1, :]
    for c in range(4):
        x, y = corner_spots(c, False)
        corner_out_a[c, 1:2, :] = flags[x, y : y + 1, :]

    loads[size_x - 1].wait()
    collide_plane(size_x - 1)
    pl.semaphore_wait(barrier, len(partners))
    copies_a[0].start()
    loads[0].wait()
    collide_plane(0)
    copies_a[1].start()
    for copy in flag_copies:
        copy.start()
    for x in range(1, size_x - 1):
        loads[x].wait()
        collide_plane(x)
    pack_rows(post_a, row_out_a, corner_out_a)
    for copy in copies_a[2:]:
        copy.start()

    tile = noise.shape[2]
    smalls[1].wait()
    smalls[2].wait()
    for g in range(patches):
        for c in range(3):
            vel_out[g, c : c + 1, :] = vel[c, g : g + 1, :]
            for t in range(beads // tile):
                span = slice(t * tile, (t + 1) * tile)
                tiled[g, t, c : c + 1, :] = pos[c, g : g + 1, span]
                tiled[g, t, c + 3 : c + 4, :] = FRICTION * vel[c, g : g + 1, span]

    vel_copies = to_group(vel_out, vel_in, vel_send, vel_recv)
    for copy in vel_copies:
        copy.start()
    vel_in[me_xs] = vel_out[me_xs]

    def bits_block(i):
        x, b = i // blocks, i % blocks
        here = block_rows(b)
        lane = lax.broadcasted_iota(jnp.int32, (8, size_z), 1)
        word = jnp.ones((8, size_z), jnp.int32)
        for k in range(1, 19):
            dirx, diry, dirz = LATTICE_DIRS[k]
            source = shift_depth(rows_behind(flags, (x + (1 - dirx),), here, diry), dirz)
            fluid = source > 0.5
            if dirz > 0:
                fluid = fluid & (lane > 0)
            elif dirz < 0:
                fluid = fluid & (lane < size_z - 1)
            word = word | jnp.where(fluid, 1 << k, 0)
        bits[x, pl.ds(here, 8), :] = word

    def pair_range(start, stop):
        def one(g):
            pair_patch(start + g, tiles, tiled, noise, force, cols, noise_t)

        repeat(stop - start, one)

    lines = size_x * size_y
    smalls[3].wait()

    def hot_patch(g):
        index = voxel[pl.ds(g, 1), :]
        hot_low[g] = one_hot(lax.rem(index, size_z), size_z)
        hot_high[g] = one_hot(lax.div(index, size_z), lines)

    repeat(patches, hot_patch, 4)

    for copy in smalls[4:]:
        copy.wait()
    early = patches // 2 - 1
    pair_range(0, early)

    for copy in flag_copies:
        copy.wait_recv()
    for copy in copies_a[2:]:
        copy.wait_recv()
    unpack_rows(post_a, row_in_a, corner_in_a)
    inside = (me_xs > 0, me_xs < n_xs - 1)
    for side in range(2):
        y = bottom if side else top
        for x in range(size_x):
            flags[x + 1, y : y + 1, :] = jnp.where(
                inside[side], row_in_a[side, 5, x : x + 1, :], 0.0
            )
    for c, k in enumerate(CORNERS):
        x, y = corner_spots(c, True)
        flags[x, y : y + 1, :] = jnp.where(
            inside[0 if LATTICE_DIRS[k][1] > 0 else 1], corner_in_a[c, 1:2, :], 0.0
        )
    repeat(size_x * blocks, bits_block, 8)

    def advance_plane(plane):
        def one_block(b):
            store_post(post_b, plane, b, collide(streamed(post_a, bits, plane, b)))

        repeat(blocks, one_block, 8)

    for plane in range(2, size_x):
        advance_plane(plane)
    copies_a[0].wait_recv()
    copies_a[1].wait_recv()
    advance_plane(size_x)
    copies_b[0].start()
    advance_plane(1)
    copies_b[1].start()
    pack_rows(post_b, row_out_b, corner_out_b)
    for copy in copies_b[2:]:
        copy.start()

    pair_range(early, patches)

    saves = [
        pltpu.make_async_copy(cells.at[:, x], pops_out.at[:, x], save_sem.at[x])
        for x in range(size_x)
    ]

    def finish_plane(plane):
        def one_block(b):
            values = streamed(post_b, bits, plane, b)
            here = block_rows(b)
            for k in range(19):
                cells[k, plane - 1, pl.ds(here, 8), :] = values[k]
            _, comps = moments(values)
            for c in range(3):
                table[plane - 1, c, pl.ds(here, 8), :] = comps[c]

        repeat(blocks, one_block, 8)
        saves[plane - 1].start()

    def gather_planes(planes, first):
        low_line, high_line = planes[0] * size_y, planes[1] * size_y
        for n, plane in enumerate(planes):
            for c in range(3):
                spot = pl.ds((2 * c + n) * size_y, size_y)
                parts[0, spot, :], parts[1, spot, :] = two_parts(table[plane, c])

        def gather_patch(g):
            line = lax.div(voxel[pl.ds(g, 1), :], size_z)
            line = jnp.where(
                line >= high_line,
                jnp.where(line < high_line + size_y, line - (high_line - size_y), -1),
                jnp.where(line < low_line + size_y, line - low_line, -1),
            )
            hit = lax.broadcasted_iota(jnp.int32, (2 * size_y, beads), 0) == line
            got = jnp.dot(parts[0], hot_low[g], preferred_element_type=F32)
            got = got + jnp.dot(parts[1], hot_low[g], preferred_element_type=F32)
            for c in range(3):
                piece = got[2 * c * size_y : 2 * (c + 1) * size_y]
                piece = VELOCITY_SCALE * jnp.where(hit, piece, 0.0).sum(axis=0, keepdims=True)
                if first:
                    flow[g, c : c + 1, :] = piece
                else:
                    flow[g, c : c + 1, :] = flow[g, c : c + 1, :] + piece

        repeat(patches, gather_patch, 4)

    for copy in copies_b[2:]:
        copy.wait_recv()
    unpack_rows(post_b, row_in_b, corner_in_b)
    finish_plane(2)
    finish_plane(3)
    gather_planes((1, 2), True)
    copies_b[0].wait_recv()
    copies_b[1].wait_recv()
    finish_plane(1)
    finish_plane(size_x)
    gather_planes((0, size_x - 1), False)
    for s in range(n_xs):
        row = jnp.int32(0)
        for g in range(patches):
            row = jnp.where(owner[g] == s, g, row)
        flow_out[s] = flow[row]
    flow_copies = to_group(flow_out, flow_in, flow_send, flow_recv)
    for copy in flow_copies:
        copy.start()
    flow_in[me_xs] = flow_out[me_xs]

    for copy in vel_copies:
        copy.wait_recv()
    def scatter_patch(g):
        reaction = -TIME_STEP * (DRAG_COEFF * (flow[g] - vel_in[owner[g]]))
        hot = hot_high[g].reshape(lines // 16, 16, beads)
        for c in range(3):
            line = jnp.broadcast_to(reaction[c : c + 1, :], (16, beads))
            for n, part in enumerate(two_parts(line)):
                scaled[n, c * lines : (c + 1) * lines, :] = (hot * part[None]).reshape(lines, beads)
        both = (((1,), (1,)), ((), ()))
        total = lax.dot_general(scaled[0], hot_low[g], both, preferred_element_type=F32)
        total = total + lax.dot_general(scaled[1], hot_low[g], both, preferred_element_type=F32)
        for c in range(3):
            field[c] = field[c] + total[c * lines : (c + 1) * lines]

    field[...] = jnp.zeros_like(field)
    repeat(patches, scatter_patch, 4)

    for copy in flow_copies:
        copy.wait_recv()
    for g in range(patches):
        drag = DRAG_COEFF * (flow_in[g] - vel_out[g])
        faster = vel_out[g] + TIME_STEP * (force[g] + drag)
        for c in range(3):
            new_vel[c, g : g + 1, :] = faster[c : c + 1, :]
    for c in range(3):
        new_pos[c] = pos[c] + TIME_STEP * new_vel[c]

    for copy in flag_copies + vel_copies + copies_a + copies_b + flow_copies:
        copy.wait_send()
    for copy in saves:
        copy.wait()


def per_device(
    n_ax, n_xs, populations, fluid_mask, patch_voxel, patch_owner, positions, velocities, pair_tiles, pair_noise
):
    size_x, size_y, size_z = fluid_mask.shape
    patches, _, beads = positions.shape
    tile = pair_noise.shape[2]
    count = beads // tile
    vmem = pl.BlockSpec(memory_space=pltpu.VMEM)
    high = size_y + 2 * PAD
    post = pltpu.VMEM((size_x + 2, 19, high, size_z), F32)
    beads3 = pltpu.VMEM((patches, 3, beads), F32)
    dma = pltpu.SemaphoreType.DMA

    def body(*refs):
        step_kernel(n_ax, n_xs, *refs)

    dist, new_pos, new_vel, field = pl.pallas_call(
        body,
        out_shape=(
            jax.ShapeDtypeStruct(populations.shape, F32),
            jax.ShapeDtypeStruct((3, patches, beads), F32),
            jax.ShapeDtypeStruct((3, patches, beads), F32),
            jax.ShapeDtypeStruct((3, size_x * size_y, size_z), F32),
        ),
        in_specs=[pl.BlockSpec(memory_space=pltpu.HBM)] * 8,
        out_specs=(pl.BlockSpec(memory_space=pl.ANY), vmem, vmem, vmem),
        scratch_shapes=[
            pltpu.SMEM((patches, 2, pair_noise.shape[1]), jnp.int32),
            pltpu.SMEM((patches,), jnp.int32),
            pltpu.VMEM((size_x, size_y, size_z), jnp.int32),
            pltpu.VMEM((patches, beads), jnp.int32),
            pltpu.VMEM((3, patches, beads), F32),
            pltpu.VMEM((3, patches, beads), F32),
            pltpu.VMEM((patches, size_z, beads), BF16),
            pltpu.VMEM((patches, size_x * size_y, beads), BF16),
            pltpu.VMEM((2, 6 * size_y, size_z), BF16),
            pltpu.VMEM(populations.shape, F32),
            post,
            post,
            pltpu.VMEM((size_x + 2, high, size_z), F32),
            pltpu.VMEM((size_x, size_y, size_z), jnp.int32),
            pltpu.VMEM(pair_noise.shape, pair_noise.dtype),
            pltpu.VMEM((2, 6, size_x, size_z), F32),
            pltpu.VMEM((2, 6, size_x, size_z), F32),
            pltpu.VMEM((4, 2, size_z), F32),
            pltpu.VMEM((4, 2, size_z), F32),
            pltpu.VMEM((2, 5, size_x, size_z), F32),
            pltpu.VMEM((2, 5, size_x, size_z), F32),
            pltpu.VMEM((4, 1, size_z), F32),
            pltpu.VMEM((4, 1, size_z), F32),
            pltpu.VMEM((2, 3 * size_x * size_y, beads), BF16),
            beads3,
            beads3,
            beads3,
            beads3,
            beads3,
            pltpu.VMEM((size_x, 3, size_y, size_z), F32),
            beads3,
            pltpu.VMEM((patches, count, 8, tile), F32),
            pltpu.VMEM((count, 6, tile, tile), F32),
            pltpu.VMEM((pair_noise.shape[1], tile, tile), F32),
            dma((size_x,)),
            dma((7,)),
            dma((size_x,)),
            dma((3, 8)),
            dma((3, 8)),
            dma((n_xs - 1,)),
            dma((n_xs - 1,)),
            dma((n_xs - 1,)),
            dma((n_xs - 1,)),
        ],
        compiler_params=pltpu.CompilerParams(
            collective_id=0, has_side_effects=True, vmem_limit_bytes=44 * 2**20
        ),
    )(
        *(
            pltpu.with_memory_space_constraint(x, pltpu.HBM)
            for x in (
                jnp.transpose(pair_tiles, (0, 2, 1)),
                patch_owner,
                populations,
                fluid_mask,
                patch_voxel,
                jnp.transpose(positions, (1, 0, 2)),
                jnp.transpose(velocities, (1, 0, 2)),
                pair_noise,
            )
        )
    )
    new_pos, new_vel = (jnp.transpose(x, (1, 0, 2)) for x in (new_pos, new_vel))
    return (dist, new_pos, new_vel, field.reshape(3, size_x, size_y, size_z))


def solution(mesh):
    n_ax, n_xs = mesh.shape["ax"], mesh.shape["xs"]

    def step(*args):
        return per_device(n_ax, n_xs, *args)

    return jax.shard_map(
        step,
        mesh=mesh,
        in_specs=(
            P(None, "ax", "xs", None),
            P("ax", "xs", None),
            P(("ax", "xs"), None),
            P(("ax", "xs")),
            P(("ax", "xs"), None, None),
            P(("ax", "xs"), None, None),
            P(("ax", "xs"), None, None),
            P(("ax", "xs"), None, None, None),
        ),
        out_specs=(
            P(None, "ax", "xs", None),
            P(("ax", "xs"), None, None),
            P(("ax", "xs"), None, None),
            P(None, "ax", "xs", None),
        ),
        check_vma=False,
    )
```

```python
import jax
import jax.numpy as jnp
from jax import lax
from jax.experimental import pallas as pl
from jax.experimental.pallas import tpu as pltpu
from jax.sharding import PartitionSpec as P

LATTICE_DIRS = [
    (0, 0, 0),
    (1, 0, 0),
    (-1, 0, 0),
    (0, 1, 0),
    (0, -1, 0),
    (0, 0, 1),
    (0, 0, -1),
    (1, 1, 0),
    (-1, -1, 0),
    (1, -1, 0),
    (-1, 1, 0),
    (1, 0, 1),
    (-1, 0, -1),
    (1, 0, -1),
    (-1, 0, 1),
    (0, 1, 1),
    (0, -1, -1),
    (0, 1, -1),
    (0, -1, 1),
]
LATTICE_WEIGHTS = [1.0 / 3.0] + [1.0 / 18.0] * 6 + [1.0 / 36.0] * 12
OPPOSITE_DIR = [0, 2, 1, 4, 3, 6, 5, 8, 7, 10, 9, 12, 11, 14, 13, 16, 15, 18, 17]
ORDER = [k for sign in (-1, 0, 1) for k in range(19) if LATTICE_DIRS[k][0] == sign]
SLOT = [ORDER.index(k) for k in range(19)]
PLUS_Y = [k for k in range(19) if LATTICE_DIRS[k][1] == 1]
MINUS_Y = [k for k in range(19) if LATTICE_DIRS[k][1] == -1]
CORNERS = [7, 8, 9, 10]
RELAX_TIME = 0.8
TIME_STEP = 0.04
REPULSION = 25.0
FRICTION = 4.5
NOISE_AMP = 3.0
NOISE_SCALE = 15.0
DRAG_COEFF = 12.5
VELOCITY_SCALE = 20.0
SOFTENING = 0.01
BF16 = jnp.bfloat16
F32 = jnp.float32
MESH = pl.DeviceIdType.MESH
PAD = 8


def moments(dist):
    density = dist[0]
    gaps = {}
    for k in range(1, 19, 2):
        density = density + (dist[k] + dist[k + 1])
        gaps[k] = dist[k] - dist[k + 1]
    inverse = 1.0 / density
    comps = []
    for axis in range(3):
        total = None
        for k in range(1, 19, 2):
            sign = LATTICE_DIRS[k][axis]
            if sign == 0:
                continue
            if total is None:
                total = gaps[k] if sign > 0 else -gaps[k]
            else:
                total = total + gaps[k] if sign > 0 else total - gaps[k]
        comps.append(total * inverse)
    return density, comps


def collide(dist):
    density, comps = moments(dist)
    base = 1.0 - 1.5 * (comps[0] * comps[0] + comps[1] * comps[1] + comps[2] * comps[2])
    gain = 1.0 / RELAX_TIME
    keep = 1.0 - gain
    out = [None] * 19
    out[0] = keep * dist[0] + (gain * LATTICE_WEIGHTS[0]) * density * base
    scaled = {w: (gain * w) * density for w in (1.0 / 18.0, 1.0 / 36.0)}
    for k in range(1, 19, 2):
        proj = None
        for axis in range(3):
            sign = LATTICE_DIRS[k][axis]
            if sign == 0:
                continue
            if proj is None:
                proj = comps[axis] if sign > 0 else -comps[axis]
            else:
                proj = proj + comps[axis] if sign > 0 else proj - comps[axis]
        amount = scaled[LATTICE_WEIGHTS[k]]
        even = amount * (base + 4.5 * (proj * proj))
        odd = amount * (3.0 * proj)
        out[k] = keep * dist[k] + (even + odd)
        out[k + 1] = keep * dist[k + 1] + (even - odd)
    return out


def shift_depth(value, amount):
    if amount == 0:
        return value
    return pltpu.roll(value, amount % value.shape[1], 1)


def block_rows(block):
    return pl.multiple_of(block * 8, 8)


def rows_behind(ref, lead, rows, amount):
    here = ref[(*lead, pl.ds(rows + PAD, 8), slice(None))]
    if amount == 0:
        return here
    sub = lax.broadcasted_iota(jnp.int32, here.shape, 0)
    beyond = ref[(*lead, pl.ds(rows + (PAD - 8 * amount), 8), slice(None))]
    mixed = jnp.where(sub == (7 if amount > 0 else 0), beyond, here)
    return pltpu.roll(mixed, amount % 8, 0)


def streamed(post, bits, plane, block):
    rows = block_rows(block)
    flags = bits[plane - 1, pl.ds(rows, 8), :]
    out = []
    for k in range(19):
        dirx, diry, dirz = LATTICE_DIRS[k]
        source = rows_behind(post, (plane - dirx, SLOT[k]), rows, diry)
        if k == 0:
            own = source
        else:
            own = post[plane, SLOT[OPPOSITE_DIR[k]], pl.ds(rows + PAD, 8), :]
        source = shift_depth(source, dirz)
        out.append(jnp.where((flags & (1 << k)) != 0, source, own))
    return out


def store_post(post, plane, block, values):
    for k in range(19):
        post[plane, SLOT[k], pl.ds(block_rows(block) + PAD, 8), :] = values[k]


def pair_patch(g, tiles, beads, noise, force, cols, noise_t):
    bead_tiles = beads.shape[1]
    pairs = noise.shape[1]
    tile = noise.shape[2]
    sub = lax.broadcasted_iota(jnp.int32, (tile, tile), 0)
    lane = lax.broadcasted_iota(jnp.int32, (tile, tile), 1)
    scaled_eye = jnp.where(sub == lane, NOISE_SCALE, 0.0).astype(BF16)
    for p in range(pairs):
        noise_t[p] = lax.dot_general(
            scaled_eye, noise[g, p], (((1,), (1,)), ((), ())), preferred_element_type=F32
        )
    for t in range(bead_tiles):
        turned = beads[g, t].T
        for c in range(6):
            cols[t, c] = jnp.broadcast_to(turned[:, c : c + 1], (tile, tile))
    step = 32

    def one_pair(p, carry):
        first, second = tiles[g, 0, p], tiles[g, 1, p]
        own = beads[g, first]
        own = [jnp.broadcast_to(own[c : c + 1, :], (step, tile)) for c in range(6)]
        sums = [None] * 3
        for start in range(0, tile, step):
            part = slice(start, start + step)
            gap = [own[c] - cols[second, c, part, :] for c in range(6)]
            dist_sq = (gap[0] * gap[0] + gap[1] * gap[1]) + (gap[2] * gap[2] + SOFTENING)
            over = jnp.maximum(0.0, lax.rsqrt(dist_sq) - 1.0)
            along = gap[0] * gap[3] + gap[1] * gap[4] + gap[2] * gap[5]
            scalar = over * ((REPULSION + noise_t[p, part, :]) - over * along)
            for c in range(3):
                piece = (scalar * gap[c]).reshape(step // 8, 8, tile).sum(axis=0)
                sums[c] = piece if sums[c] is None else sums[c] + piece
        out = []
        for t in range(bead_tiles):
            for c in range(3):
                out.append(carry[t * 3 + c] + jnp.where(first == t, sums[c], 0.0))
        return tuple(out)

    def two_pairs(p, carry):
        return one_pair(2 * p + 1, one_pair(2 * p, carry))

    zero = jnp.zeros((8, tile), F32)
    total = lax.fori_loop(0, pairs // 2, two_pairs, (zero,) * (3 * bead_tiles))
    for t in range(bead_tiles):
        for c in range(3):
            force[g, c : c + 1, t * tile : (t + 1) * tile] = total[t * 3 + c].sum(
                axis=0, keepdims=True
            )


def two_parts(value):
    high = value.astype(BF16)
    return high, (value - high.astype(F32)).astype(BF16)


def one_hot(index, size):
    beads = index.shape[1]
    rows = lax.broadcasted_iota(jnp.int32, (size, beads), 0)
    return jnp.where(rows == index, 1.0, 0.0).astype(BF16)


def repeat(count, body, together=1):
    def turn(i, carry):
        for n in range(together):
            body(i * together + n)
        return carry

    lax.fori_loop(0, count // together, turn, 0)


def step_kernel(
    n_ax,
    n_xs,
    tiles_hbm,
    owner_hbm,
    pops,
    mask_hbm,
    voxel_hbm,
    pos_hbm,
    vel_hbm,
    noise_hbm,
    pops_out,
    new_pos,
    new_vel,
    field,
    tiles,
    owner,
    mask,
    voxel,
    pos,
    vel,
    hot_low,
    hot_high,
    parts,
    cells,
    post_a,
    post_b,
    flags,
    bits,
    noise,
    row_out_a,
    row_in_a,
    corner_out_a,
    corner_in_a,
    row_out_b,
    row_in_b,
    corner_out_b,
    corner_in_b,
    scaled,
    vel_in,
    flow,
    flow_out,
    flow_in,
    force,
    table,
    vel_out,
    tiled,
    cols,
    noise_t,
    load_sem,
    small_sem,
    save_sem,
    near_send,
    near_recv,
    vel_send,
    vel_recv,
    flow_send,
    flow_recv,
):
    size_x, size_y, size_z = mask_hbm.shape
    blocks = size_y // 8
    top, bottom = PAD - 1, PAD + size_y
    first_row, last_row = PAD, PAD + size_y - 1
    own_rows = pl.ds(PAD, size_y)
    _, patches, beads = pos_hbm.shape
    me_ax, me_xs = lax.axis_index("ax"), lax.axis_index("xs")

    def at(move_ax, move_xs):
        return (lax.rem(me_ax + (move_ax + n_ax), n_ax), lax.rem(me_xs + (move_xs + n_xs), n_xs))

    loads = [
        pltpu.make_async_copy(pops.at[:, x], cells.at[:, x], load_sem.at[x]) for x in range(size_x)
    ]
    smalls = [
        pltpu.make_async_copy(src, dst, small_sem.at[i])
        for i, (src, dst) in enumerate(
            [
                (mask_hbm, mask),
                (pos_hbm, pos),
                (vel_hbm, vel),
                (voxel_hbm, voxel),
                (tiles_hbm, tiles),
                (owner_hbm, owner),
                (noise_hbm, noise),
            ]
        )
    ]
    loads[size_x - 1].start()
    loads[0].start()
    for copy in smalls[:-1]:
        copy.start()
    for x in range(1, size_x - 1):
        loads[x].start()
    smalls[-1].start()

    partners = [at(1, 0), at(-1, 0)] + [at(0, d) for d in range(1, n_xs)]
    partners += [at(a, b) for a in (1, -1) for b in (1, -1)]
    barrier = pltpu.get_barrier_semaphore()
    for partner in partners:
        pl.semaphore_signal(barrier, inc=1, device_id=partner, device_id_type=MESH)

    def remote(src, dst, sems, spot, target):
        return pltpu.make_async_remote_copy(
            src_ref=src,
            dst_ref=dst,
            send_sem=sems[0].at[spot],
            recv_sem=sems[1].at[spot],
            device_id=target,
            device_id_type=MESH,
        )

    near = (near_send, near_recv)
    flag_copies = [
        remote(flags.at[size_x, own_rows], flags.at[0, own_rows], near, (0, 0), at(1, 0)),
        remote(flags.at[1, own_rows], flags.at[size_x + 1, own_rows], near, (0, 1), at(-1, 0)),
    ]

    def to_group(source, target, send, recv):
        return [
            pltpu.make_async_remote_copy(
                src_ref=source.at[at(0, d)[1]],
                dst_ref=target.at[me_xs],
                send_sem=send.at[d - 1],
                recv_sem=recv.at[d - 1],
                device_id=at(0, d),
                device_id_type=MESH,
            )
            for d in range(1, n_xs)
        ]

    def post_copies(part, post, row_bufs, corner_bufs):
        ends = [
            (post.at[size_x, 14:19, own_rows], post.at[0, 14:19, own_rows], at(1, 0)),
            (post.at[1, 0:5, own_rows], post.at[size_x + 1, 0:5, own_rows], at(-1, 0)),
        ]
        for side in range(2):
            ends.append((row_bufs[0].at[side], row_bufs[1].at[side], at(0, 1 - 2 * side)))
        for c, k in enumerate(CORNERS):
            target = at(LATTICE_DIRS[k][0], LATTICE_DIRS[k][1])
            ends.append((corner_bufs[0].at[c], corner_bufs[1].at[c], target))
        return [
            remote(src, dst, near, (part, i), target) for i, (src, dst, target) in enumerate(ends)
        ]

    def corner_spots(c, halo):
        dirx, diry, _ = LATTICE_DIRS[CORNERS[c]]
        if halo:
            return (0 if dirx > 0 else size_x + 1), (top if diry > 0 else bottom)
        return (size_x if dirx > 0 else 1), (last_row if diry > 0 else first_row)

    def pack_rows(post, row_buf, corner_buf):
        for side, dirs in enumerate((PLUS_Y, MINUS_Y)):
            y = first_row if side else last_row
            for i, k in enumerate(dirs):
                for x in range(size_x):
                    row_buf[side, i, x : x + 1, :] = post[x + 1, SLOT[k], y : y + 1, :]
        for c, k in enumerate(CORNERS):
            x, y = corner_spots(c, False)
            corner_buf[c, 0:1, :] = post[x, SLOT[k], y : y + 1, :]

    def unpack_rows(post, row_buf, corner_buf):
        for side, dirs in enumerate((PLUS_Y, MINUS_Y)):
            y = bottom if side else top
            for i, k in enumerate(dirs):
                for x in range(size_x):
                    post[x + 1, SLOT[k], y : y + 1, :] = row_buf[side, i, x : x + 1, :]
        for c, k in enumerate(CORNERS):
            x, y = corner_spots(c, True)
            post[x, SLOT[k], y : y + 1, :] = corner_buf[c, 0:1, :]

    def collide_plane(x):
        def one_block(b):
            values = collide([cells[k, x, pl.ds(block_rows(b), 8), :] for k in range(19)])
            store_post(post_a, x + 1, b, values)

        repeat(blocks, one_block, 8)

    rows_a, corners_a = (row_out_a, row_in_a), (corner_out_a, corner_in_a)
    rows_b, corners_b = (row_out_b, row_in_b), (corner_out_b, corner_in_b)
    copies_a = post_copies(1, post_a, rows_a, corners_a)
    copies_b = post_copies(2, post_b, rows_b, corners_b)

    smalls[0].wait()
    for x in range(size_x):
        plane = mask[x].astype(F32)
        flags[x + 1, own_rows, :] = plane
        row_out_a[0, 5, x : x + 1, :] = plane[size_y - 1 : size_y, :]
        row_out_a[1, 5, x : x + 1, :] = plane[0:1, :]
    for c in range(4):
        x, y = corner_spots(c, False)
        corner_out_a[c, 1:2, :] = flags[x, y : y + 1, :]

    loads[size_x - 1].wait()
    collide_plane(size_x - 1)
    pl.semaphore_wait(barrier, len(partners))
    copies_a[0].start()
    loads[0].wait()
    collide_plane(0)
    copies_a[1].start()
    for copy in flag_copies:
        copy.start()
    for x in range(1, size_x - 1):
        loads[x].wait()
        collide_plane(x)
    pack_rows(post_a, row_out_a, corner_out_a)
    for copy in copies_a[2:]:
        copy.start()

    tile = noise.shape[2]
    smalls[1].wait()
    smalls[2].wait()
    for g in range(patches):
        for c in range(3):
            vel_out[g, c : c + 1, :] = vel[c, g : g + 1, :]
            for t in range(beads // tile):
                span = slice(t * tile, (t + 1) * tile)
                tiled[g, t, c : c + 1, :] = pos[c, g : g + 1, span]
                tiled[g, t, c + 3 : c + 4, :] = FRICTION * vel[c, g : g + 1, span]

    vel_copies = to_group(vel_out, vel_in, vel_send, vel_recv)
    for copy in vel_copies:
        copy.start()
    vel_in[me_xs] = vel_out[me_xs]

    def bits_block(i):
        x, b = i // blocks, i % blocks
        here = block_rows(b)
        lane = lax.broadcasted_iota(jnp.int32, (8, size_z), 1)
        word = jnp.ones((8, size_z), jnp.int32)
        for k in range(1, 19):
            dirx, diry, dirz = LATTICE_DIRS[k]
            source = shift_depth(rows_behind(flags, (x + (1 - dirx),), here, diry), dirz)
            fluid = source > 0.5
            if dirz > 0:
                fluid = fluid & (lane > 0)
            elif dirz < 0:
                fluid = fluid & (lane < size_z - 1)
            word = word | jnp.where(fluid, 1 << k, 0)
        bits[x, pl.ds(here, 8), :] = word

    def pair_range(start, stop):
        def one(g):
            pair_patch(start + g, tiles, tiled, noise, force, cols, noise_t)

        repeat(stop - start, one)

    lines = size_x * size_y
    smalls[3].wait()

    def hot_patch(g):
        index = voxel[pl.ds(g, 1), :]
        hot_low[g] = one_hot(lax.rem(index, size_z), size_z)
        hot_high[g] = one_hot(lax.div(index, size_z), lines)

    repeat(patches, hot_patch, 4)

    for copy in smalls[4:]:
        copy.wait()
    early = patches // 2 + 1
    pair_range(0, early)

    for copy in flag_copies:
        copy.wait_recv()
    for copy in copies_a[2:]:
        copy.wait_recv()
    unpack_rows(post_a, row_in_a, corner_in_a)
    inside = (me_xs > 0, me_xs < n_xs - 1)
    for side in range(2):
        y = bottom if side else top
        for x in range(size_x):
            flags[x + 1, y : y + 1, :] = jnp.where(
                inside[side], row_in_a[side, 5, x : x + 1, :], 0.0
            )
    for c, k in enumerate(CORNERS):
        x, y = corner_spots(c, True)
        flags[x, y : y + 1, :] = jnp.where(
            inside[0 if LATTICE_DIRS[k][1] > 0 else 1], corner_in_a[c, 1:2, :], 0.0
        )
    repeat(size_x * blocks, bits_block, 8)

    def advance_plane(plane):
        def one_block(b):
            store_post(post_b, plane, b, collide(streamed(post_a, bits, plane, b)))

        repeat(blocks, one_block, 8)

    for plane in range(2, size_x):
        advance_plane(plane)
    copies_a[0].wait_recv()
    copies_a[1].wait_recv()
    advance_plane(size_x)
    copies_b[0].start()
    advance_plane(1)
    copies_b[1].start()
    pack_rows(post_b, row_out_b, corner_out_b)
    for copy in copies_b[2:]:
        copy.start()

    pair_range(early, patches)

    saves = [
        pltpu.make_async_copy(cells.at[:, x], pops_out.at[:, x], save_sem.at[x])
        for x in range(size_x)
    ]

    def finish_plane(plane):
        def one_block(b):
            values = streamed(post_b, bits, plane, b)
            here = block_rows(b)
            for k in range(19):
                cells[k, plane - 1, pl.ds(here, 8), :] = values[k]
            _, comps = moments(values)
            for c in range(3):
                table[plane - 1, c, pl.ds(here, 8), :] = comps[c]

        repeat(blocks, one_block, 8)
        saves[plane - 1].start()

    def gather_planes(planes, first):
        low_line, high_line = planes[0] * size_y, planes[1] * size_y
        for n, plane in enumerate(planes):
            for c in range(3):
                spot = pl.ds((2 * c + n) * size_y, size_y)
                parts[0, spot, :], parts[1, spot, :] = two_parts(table[plane, c])

        def gather_patch(g):
            line = lax.div(voxel[pl.ds(g, 1), :], size_z)
            line = jnp.where(
                line >= high_line,
                jnp.where(line < high_line + size_y, line - (high_line - size_y), -1),
                jnp.where(line < low_line + size_y, line - low_line, -1),
            )
            hit = lax.broadcasted_iota(jnp.int32, (2 * size_y, beads), 0) == line
            got = jnp.dot(parts[0], hot_low[g], preferred_element_type=F32)
            got = got + jnp.dot(parts[1], hot_low[g], preferred_element_type=F32)
            for c in range(3):
                piece = got[2 * c * size_y : 2 * (c + 1) * size_y]
                piece = VELOCITY_SCALE * jnp.where(hit, piece, 0.0).sum(axis=0, keepdims=True)
                if first:
                    flow[g, c : c + 1, :] = piece
                else:
                    flow[g, c : c + 1, :] = flow[g, c : c + 1, :] + piece

        repeat(patches, gather_patch, 4)

    for copy in copies_b[2:]:
        copy.wait_recv()
    unpack_rows(post_b, row_in_b, corner_in_b)
    finish_plane(2)
    finish_plane(3)
    gather_planes((1, 2), True)
    copies_b[0].wait_recv()
    copies_b[1].wait_recv()
    finish_plane(1)
    finish_plane(size_x)
    gather_planes((0, size_x - 1), False)
    for s in range(n_xs):
        row = jnp.int32(0)
        for g in range(patches):
            row = jnp.where(owner[g] == s, g, row)
        flow_out[s] = flow[row]
    flow_copies = to_group(flow_out, flow_in, flow_send, flow_recv)
    for copy in flow_copies:
        copy.start()
    flow_in[me_xs] = flow_out[me_xs]

    for copy in vel_copies:
        copy.wait_recv()
    def scatter_patch(g):
        reaction = -TIME_STEP * (DRAG_COEFF * (flow[g] - vel_in[owner[g]]))
        hot = hot_high[g].reshape(lines // 16, 16, beads)
        for c in range(3):
            line = jnp.broadcast_to(reaction[c : c + 1, :], (16, beads))
            for n, part in enumerate(two_parts(line)):
                scaled[n, c * lines : (c + 1) * lines, :] = (hot * part[None]).reshape(lines, beads)
        both = (((1,), (1,)), ((), ()))
        total = lax.dot_general(scaled[0], hot_low[g], both, preferred_element_type=F32)
        total = total + lax.dot_general(scaled[1], hot_low[g], both, preferred_element_type=F32)
        for c in range(3):
            field[c] = field[c] + total[c * lines : (c + 1) * lines]

    field[...] = jnp.zeros_like(field)
    repeat(patches, scatter_patch, 4)

    for copy in flow_copies:
        copy.wait_recv()
    for g in range(patches):
        drag = DRAG_COEFF * (flow_in[g] - vel_out[g])
        faster = vel_out[g] + TIME_STEP * (force[g] + drag)
        for c in range(3):
            new_vel[c, g : g + 1, :] = faster[c : c + 1, :]
    for c in range(3):
        new_pos[c] = pos[c] + TIME_STEP * new_vel[c]

    for copy in flag_copies + vel_copies + copies_a + copies_b + flow_copies:
        copy.wait_send()
    for copy in saves:
        copy.wait()


def per_device(
    n_ax, n_xs, populations, fluid_mask, patch_voxel, patch_owner, positions, velocities, pair_tiles, pair_noise
):
    size_x, size_y, size_z = fluid_mask.shape
    patches, _, beads = positions.shape
    tile = pair_noise.shape[2]
    count = beads // tile
    vmem = pl.BlockSpec(memory_space=pltpu.VMEM)
    high = size_y + 2 * PAD
    post = pltpu.VMEM((size_x + 2, 19, high, size_z), F32)
    beads3 = pltpu.VMEM((patches, 3, beads), F32)
    dma = pltpu.SemaphoreType.DMA

    def body(*refs):
        step_kernel(n_ax, n_xs, *refs)

    dist, new_pos, new_vel, field = pl.pallas_call(
        body,
        out_shape=(
            jax.ShapeDtypeStruct(populations.shape, F32),
            jax.ShapeDtypeStruct((3, patches, beads), F32),
            jax.ShapeDtypeStruct((3, patches, beads), F32),
            jax.ShapeDtypeStruct((3, size_x * size_y, size_z), F32),
        ),
        in_specs=[pl.BlockSpec(memory_space=pltpu.HBM)] * 8,
        out_specs=(pl.BlockSpec(memory_space=pl.ANY), vmem, vmem, vmem),
        scratch_shapes=[
            pltpu.SMEM((patches, 2, pair_noise.shape[1]), jnp.int32),
            pltpu.SMEM((patches,), jnp.int32),
            pltpu.VMEM((size_x, size_y, size_z), jnp.int32),
            pltpu.VMEM((patches, beads), jnp.int32),
            pltpu.VMEM((3, patches, beads), F32),
            pltpu.VMEM((3, patches, beads), F32),
            pltpu.VMEM((patches, size_z, beads), BF16),
            pltpu.VMEM((patches, size_x * size_y, beads), BF16),
            pltpu.VMEM((2, 6 * size_y, size_z), BF16),
            pltpu.VMEM(populations.shape, F32),
            post,
            post,
            pltpu.VMEM((size_x + 2, high, size_z), F32),
            pltpu.VMEM((size_x, size_y, size_z), jnp.int32),
            pltpu.VMEM(pair_noise.shape, pair_noise.dtype),
            pltpu.VMEM((2, 6, size_x, size_z), F32),
            pltpu.VMEM((2, 6, size_x, size_z), F32),
            pltpu.VMEM((4, 2, size_z), F32),
            pltpu.VMEM((4, 2, size_z), F32),
            pltpu.VMEM((2, 5, size_x, size_z), F32),
            pltpu.VMEM((2, 5, size_x, size_z), F32),
            pltpu.VMEM((4, 1, size_z), F32),
            pltpu.VMEM((4, 1, size_z), F32),
            pltpu.VMEM((2, 3 * size_x * size_y, beads), BF16),
            beads3,
            beads3,
            beads3,
            beads3,
            beads3,
            pltpu.VMEM((size_x, 3, size_y, size_z), F32),
            beads3,
            pltpu.VMEM((patches, count, 8, tile), F32),
            pltpu.VMEM((count, 6, tile, tile), F32),
            pltpu.VMEM((pair_noise.shape[1], tile, tile), F32),
            dma((size_x,)),
            dma((7,)),
            dma((size_x,)),
            dma((3, 8)),
            dma((3, 8)),
            dma((n_xs - 1,)),
            dma((n_xs - 1,)),
            dma((n_xs - 1,)),
            dma((n_xs - 1,)),
        ],
        compiler_params=pltpu.CompilerParams(
            collective_id=0, has_side_effects=True, vmem_limit_bytes=44 * 2**20
        ),
    )(
        *(
            pltpu.with_memory_space_constraint(x, pltpu.HBM)
            for x in (
                jnp.transpose(pair_tiles, (0, 2, 1)),
                patch_owner,
                populations,
                fluid_mask,
                patch_voxel,
                jnp.transpose(positions, (1, 0, 2)),
                jnp.transpose(velocities, (1, 0, 2)),
                pair_noise,
            )
        )
    )
    new_pos, new_vel = (jnp.transpose(x, (1, 0, 2)) for x in (new_pos, new_vel))
    return (dist, new_pos, new_vel, field.reshape(3, size_x, size_y, size_z))


def solution(mesh):
    n_ax, n_xs = mesh.shape["ax"], mesh.shape["xs"]

    def step(*args):
        return per_device(n_ax, n_xs, *args)

    return jax.shard_map(
        step,
        mesh=mesh,
        in_specs=(
            P(None, "ax", "xs", None),
            P("ax", "xs", None),
            P(("ax", "xs"), None),
            P(("ax", "xs")),
            P(("ax", "xs"), None, None),
            P(("ax", "xs"), None, None),
            P(("ax", "xs"), None, None),
            P(("ax", "xs"), None, None, None),
        ),
        out_specs=(
            P(None, "ax", "xs", None),
            P(("ax", "xs"), None, None),
            P(("ax", "xs"), None, None),
            P(None, "ax", "xs", None),
        ),
        check_vma=False,
    )
```

```python
import jax
import jax.numpy as jnp
from jax import lax
from jax.experimental import pallas as pl
from jax.experimental.pallas import tpu as pltpu
from jax.sharding import PartitionSpec as P

LATTICE_DIRS = [
    (0, 0, 0),
    (1, 0, 0),
    (-1, 0, 0),
    (0, 1, 0),
    (0, -1, 0),
    (0, 0, 1),
    (0, 0, -1),
    (1, 1, 0),
    (-1, -1, 0),
    (1, -1, 0),
    (-1, 1, 0),
    (1, 0, 1),
    (-1, 0, -1),
    (1, 0, -1),
    (-1, 0, 1),
    (0, 1, 1),
    (0, -1, -1),
    (0, 1, -1),
    (0, -1, 1),
]
LATTICE_WEIGHTS = [1.0 / 3.0] + [1.0 / 18.0] * 6 + [1.0 / 36.0] * 12
OPPOSITE_DIR = [0, 2, 1, 4, 3, 6, 5, 8, 7, 10, 9, 12, 11, 14, 13, 16, 15, 18, 17]
ORDER = [k for sign in (-1, 0, 1) for k in range(19) if LATTICE_DIRS[k][0] == sign]
SLOT = [ORDER.index(k) for k in range(19)]
PLUS_Y = [k for k in range(19) if LATTICE_DIRS[k][1] == 1]
MINUS_Y = [k for k in range(19) if LATTICE_DIRS[k][1] == -1]
CORNERS = [7, 8, 9, 10]
RELAX_TIME = 0.8
TIME_STEP = 0.04
REPULSION = 25.0
FRICTION = 4.5
NOISE_AMP = 3.0
NOISE_SCALE = 15.0
DRAG_COEFF = 12.5
VELOCITY_SCALE = 20.0
SOFTENING = 0.01
BF16 = jnp.bfloat16
F32 = jnp.float32
MESH = pl.DeviceIdType.MESH
PAD = 8


def moments(dist):
    density = dist[0]
    gaps = {}
    for k in range(1, 19, 2):
        density = density + (dist[k] + dist[k + 1])
        gaps[k] = dist[k] - dist[k + 1]
    inverse = 1.0 / density
    comps = []
    for axis in range(3):
        total = None
        for k in range(1, 19, 2):
            sign = LATTICE_DIRS[k][axis]
            if sign == 0:
                continue
            if total is None:
                total = gaps[k] if sign > 0 else -gaps[k]
            else:
                total = total + gaps[k] if sign > 0 else total - gaps[k]
        comps.append(total * inverse)
    return density, comps


def collide(dist):
    density, comps = moments(dist)
    base = 1.0 - 1.5 * (comps[0] * comps[0] + comps[1] * comps[1] + comps[2] * comps[2])
    gain = 1.0 / RELAX_TIME
    keep = 1.0 - gain
    out = [None] * 19
    out[0] = keep * dist[0] + (gain * LATTICE_WEIGHTS[0]) * density * base
    scaled = {w: (gain * w) * density for w in (1.0 / 18.0, 1.0 / 36.0)}
    for k in range(1, 19, 2):
        proj = None
        for axis in range(3):
            sign = LATTICE_DIRS[k][axis]
            if sign == 0:
                continue
            if proj is None:
                proj = comps[axis] if sign > 0 else -comps[axis]
            else:
                proj = proj + comps[axis] if sign > 0 else proj - comps[axis]
        amount = scaled[LATTICE_WEIGHTS[k]]
        even = amount * (base + 4.5 * (proj * proj))
        odd = amount * (3.0 * proj)
        out[k] = keep * dist[k] + (even + odd)
        out[k + 1] = keep * dist[k + 1] + (even - odd)
    return out


def shift_depth(value, amount):
    if amount == 0:
        return value
    return pltpu.roll(value, amount % value.shape[1], 1)


def block_rows(block):
    return pl.multiple_of(block * 8, 8)


def rows_behind(ref, lead, rows, amount):
    here = ref[(*lead, pl.ds(rows + PAD, 8), slice(None))]
    if amount == 0:
        return here
    sub = lax.broadcasted_iota(jnp.int32, here.shape, 0)
    beyond = ref[(*lead, pl.ds(rows + (PAD - 8 * amount), 8), slice(None))]
    mixed = jnp.where(sub == (7 if amount > 0 else 0), beyond, here)
    return pltpu.roll(mixed, amount % 8, 0)


def streamed(post, bits, plane, block):
    rows = block_rows(block)
    flags = bits[plane - 1, pl.ds(rows, 8), :]
    out = []
    for k in range(19):
        dirx, diry, dirz = LATTICE_DIRS[k]
        source = rows_behind(post, (plane - dirx, SLOT[k]), rows, diry)
        if k == 0:
            own = source
        else:
            own = post[plane, SLOT[OPPOSITE_DIR[k]], pl.ds(rows + PAD, 8), :]
        source = shift_depth(source, dirz)
        out.append(jnp.where((flags & (1 << k)) != 0, source, own))
    return out


def store_post(post, plane, block, values):
    for k in range(19):
        post[plane, SLOT[k], pl.ds(block_rows(block) + PAD, 8), :] = values[k]


def pair_patch(g, tiles, beads, noise, force, cols, noise_t):
    bead_tiles = beads.shape[1]
    pairs = noise.shape[1]
    tile = noise.shape[2]
    sub = lax.broadcasted_iota(jnp.int32, (tile, tile), 0)
    lane = lax.broadcasted_iota(jnp.int32, (tile, tile), 1)
    scaled_eye = jnp.where(sub == lane, NOISE_SCALE, 0.0).astype(BF16)
    for p in range(pairs):
        noise_t[p] = lax.dot_general(
            scaled_eye, noise[g, p], (((1,), (1,)), ((), ())), preferred_element_type=F32
        )
    for t in range(bead_tiles):
        turned = beads[g, t].T
        for c in range(6):
            cols[t, c] = jnp.broadcast_to(turned[:, c : c + 1], (tile, tile))
    step = 32

    def one_pair(p, carry):
        first, second = tiles[g, 0, p], tiles[g, 1, p]
        own = beads[g, first]
        own = [jnp.broadcast_to(own[c : c + 1, :], (step, tile)) for c in range(6)]
        sums = [None] * 3
        for start in range(0, tile, step):
            part = slice(start, start + step)
            gap = [own[c] - cols[second, c, part, :] for c in range(6)]
            dist_sq = (gap[0] * gap[0] + gap[1] * gap[1]) + (gap[2] * gap[2] + SOFTENING)
            over = jnp.maximum(0.0, lax.rsqrt(dist_sq) - 1.0)
            along = gap[0] * gap[3] + gap[1] * gap[4] + gap[2] * gap[5]
            scalar = over * ((REPULSION + noise_t[p, part, :]) - over * along)
            for c in range(3):
                piece = (scalar * gap[c]).reshape(step // 8, 8, tile).sum(axis=0)
                sums[c] = piece if sums[c] is None else sums[c] + piece
        out = []
        for t in range(bead_tiles):
            for c in range(3):
                out.append(carry[t * 3 + c] + jnp.where(first == t, sums[c], 0.0))
        return tuple(out)

    def two_pairs(p, carry):
        return one_pair(2 * p + 1, one_pair(2 * p, carry))

    zero = jnp.zeros((8, tile), F32)
    total = lax.fori_loop(0, pairs // 2, two_pairs, (zero,) * (3 * bead_tiles))
    for t in range(bead_tiles):
        for c in range(3):
            force[g, c : c + 1, t * tile : (t + 1) * tile] = total[t * 3 + c].sum(
                axis=0, keepdims=True
            )


def two_parts(value):
    high = value.astype(BF16)
    return high, (value - high.astype(F32)).astype(BF16)


def one_hot(index, size):
    beads = index.shape[1]
    rows = lax.broadcasted_iota(jnp.int32, (size, beads), 0)
    return jnp.where(rows == index, 1.0, 0.0).astype(BF16)


def repeat(count, body, together=1):
    def turn(i, carry):
        for n in range(together):
            body(i * together + n)
        return carry

    lax.fori_loop(0, count // together, turn, 0)


def step_kernel(
    n_ax,
    n_xs,
    tiles_hbm,
    owner_hbm,
    pops,
    mask_hbm,
    voxel_hbm,
    pos_hbm,
    vel_hbm,
    noise_hbm,
    pops_out,
    new_pos,
    new_vel,
    field,
    tiles,
    owner,
    mask,
    voxel,
    pos,
    vel,
    hot_low,
    hot_high,
    parts,
    cells,
    post_a,
    post_b,
    flags,
    bits,
    noise,
    row_out_a,
    row_in_a,
    corner_out_a,
    corner_in_a,
    row_out_b,
    row_in_b,
    corner_out_b,
    corner_in_b,
    scaled,
    vel_in,
    flow,
    flow_out,
    flow_in,
    force,
    table,
    vel_out,
    tiled,
    cols,
    noise_t,
    load_sem,
    small_sem,
    save_sem,
    near_send,
    near_recv,
    vel_send,
    vel_recv,
    flow_send,
    flow_recv,
):
    size_x, size_y, size_z = mask_hbm.shape
    blocks = size_y // 8
    top, bottom = PAD - 1, PAD + size_y
    first_row, last_row = PAD, PAD + size_y - 1
    own_rows = pl.ds(PAD, size_y)
    _, patches, beads = pos_hbm.shape
    me_ax, me_xs = lax.axis_index("ax"), lax.axis_index("xs")

    def at(move_ax, move_xs):
        return (lax.rem(me_ax + (move_ax + n_ax), n_ax), lax.rem(me_xs + (move_xs + n_xs), n_xs))

    loads = [
        pltpu.make_async_copy(pops.at[:, x], cells.at[:, x], load_sem.at[x]) for x in range(size_x)
    ]
    smalls = [
        pltpu.make_async_copy(src, dst, small_sem.at[i])
        for i, (src, dst) in enumerate(
            [
                (mask_hbm, mask),
                (pos_hbm, pos),
                (vel_hbm, vel),
                (voxel_hbm, voxel),
                (tiles_hbm, tiles),
                (owner_hbm, owner),
                (noise_hbm, noise),
            ]
        )
    ]
    loads[size_x - 1].start()
    loads[0].start()
    for copy in smalls[:-1]:
        copy.start()
    for x in range(1, size_x - 1):
        loads[x].start()
    smalls[-1].start()

    partners = [at(1, 0), at(-1, 0)] + [at(0, d) for d in range(1, n_xs)]
    partners += [at(a, b) for a in (1, -1) for b in (1, -1)]
    barrier = pltpu.get_barrier_semaphore()
    for partner in partners:
        pl.semaphore_signal(barrier, inc=1, device_id=partner, device_id_type=MESH)

    def remote(src, dst, sems, spot, target):
        return pltpu.make_async_remote_copy(
            src_ref=src,
            dst_ref=dst,
            send_sem=sems[0].at[spot],
            recv_sem=sems[1].at[spot],
            device_id=target,
            device_id_type=MESH,
        )

    near = (near_send, near_recv)
    flag_copies = [
        remote(flags.at[size_x, own_rows], flags.at[0, own_rows], near, (0, 0), at(1, 0)),
        remote(flags.at[1, own_rows], flags.at[size_x + 1, own_rows], near, (0, 1), at(-1, 0)),
    ]

    def to_group(source, target, send, recv):
        return [
            pltpu.make_async_remote_copy(
                src_ref=source.at[at(0, d)[1]],
                dst_ref=target.at[me_xs],
                send_sem=send.at[d - 1],
                recv_sem=recv.at[d - 1],
                device_id=at(0, d),
                device_id_type=MESH,
            )
            for d in range(1, n_xs)
        ]

    def post_copies(part, post, row_bufs, corner_bufs):
        ends = [
            (post.at[size_x, 14:19, own_rows], post.at[0, 14:19, own_rows], at(1, 0)),
            (post.at[1, 0:5, own_rows], post.at[size_x + 1, 0:5, own_rows], at(-1, 0)),
        ]
        for side in range(2):
            ends.append((row_bufs[0].at[side], row_bufs[1].at[side], at(0, 1 - 2 * side)))
        for c, k in enumerate(CORNERS):
            target = at(LATTICE_DIRS[k][0], LATTICE_DIRS[k][1])
            ends.append((corner_bufs[0].at[c], corner_bufs[1].at[c], target))
        return [
            remote(src, dst, near, (part, i), target) for i, (src, dst, target) in enumerate(ends)
        ]

    def corner_spots(c, halo):
        dirx, diry, _ = LATTICE_DIRS[CORNERS[c]]
        if halo:
            return (0 if dirx > 0 else size_x + 1), (top if diry > 0 else bottom)
        return (size_x if dirx > 0 else 1), (last_row if diry > 0 else first_row)

    def pack_rows(post, row_buf, corner_buf):
        for side, dirs in enumerate((PLUS_Y, MINUS_Y)):
            y = first_row if side else last_row
            for i, k in enumerate(dirs):
                for x in range(size_x):
                    row_buf[side, i, x : x + 1, :] = post[x + 1, SLOT[k], y : y + 1, :]
        for c, k in enumerate(CORNERS):
            x, y = corner_spots(c, False)
            corner_buf[c, 0:1, :] = post[x, SLOT[k], y : y + 1, :]

    def unpack_rows(post, row_buf, corner_buf):
        for side, dirs in enumerate((PLUS_Y, MINUS_Y)):
            y = bottom if side else top
            for i, k in enumerate(dirs):
                for x in range(size_x):
                    post[x + 1, SLOT[k], y : y + 1, :] = row_buf[side, i, x : x + 1, :]
        for c, k in enumerate(CORNERS):
            x, y = corner_spots(c, True)
            post[x, SLOT[k], y : y + 1, :] = corner_buf[c, 0:1, :]

    def collide_plane(x):
        def one_block(b):
            values = collide([cells[k, x, pl.ds(block_rows(b), 8), :] for k in range(19)])
            store_post(post_a, x + 1, b, values)

        repeat(blocks, one_block, 8)

    rows_a, corners_a = (row_out_a, row_in_a), (corner_out_a, corner_in_a)
    rows_b, corners_b = (row_out_b, row_in_b), (corner_out_b, corner_in_b)
    copies_a = post_copies(1, post_a, rows_a, corners_a)
    copies_b = post_copies(2, post_b, rows_b, corners_b)

    smalls[0].wait()
    for x in range(size_x):
        plane = mask[x].astype(F32)
        flags[x + 1, own_rows, :] = plane
        row_out_a[0, 5, x : x + 1, :] = plane[size_y - 1 : size_y, :]
        row_out_a[1, 5, x : x + 1, :] = plane[0:1, :]
    for c in range(4):
        x, y = corner_spots(c, False)
        corner_out_a[c, 1:2, :] = flags[x, y : y + 1, :]

    loads[size_x - 1].wait()
    collide_plane(size_x - 1)
    pl.semaphore_wait(barrier, len(partners))
    copies_a[0].start()
    loads[0].wait()
    collide_plane(0)
    copies_a[1].start()
    for copy in flag_copies:
        copy.start()
    for x in range(1, size_x - 1):
        loads[x].wait()
        collide_plane(x)
    pack_rows(post_a, row_out_a, corner_out_a)
    for copy in copies_a[2:]:
        copy.start()

    tile = noise.shape[2]
    smalls[1].wait()
    smalls[2].wait()
    for g in range(patches):
        for c in range(3):
            vel_out[g, c : c + 1, :] = vel[c, g : g + 1, :]
            for t in range(beads // tile):
                span = slice(t * tile, (t + 1) * tile)
                tiled[g, t, c : c + 1, :] = pos[c, g : g + 1, span]
                tiled[g, t, c + 3 : c + 4, :] = FRICTION * vel[c, g : g + 1, span]

    vel_copies = to_group(vel_out, vel_in, vel_send, vel_recv)
    for copy in vel_copies:
        copy.start()
    vel_in[me_xs] = vel_out[me_xs]

    def bits_block(i):
        x, b = i // blocks, i % blocks
        here = block_rows(b)
        lane = lax.broadcasted_iota(jnp.int32, (8, size_z), 1)
        word = jnp.ones((8, size_z), jnp.int32)
        for k in range(1, 19):
            dirx, diry, dirz = LATTICE_DIRS[k]
            source = shift_depth(rows_behind(flags, (x + (1 - dirx),), here, diry), dirz)
            fluid = source > 0.5
            if dirz > 0:
                fluid = fluid & (lane > 0)
            elif dirz < 0:
                fluid = fluid & (lane < size_z - 1)
            word = word | jnp.where(fluid, 1 << k, 0)
        bits[x, pl.ds(here, 8), :] = word

    def pair_range(start, stop):
        def one(g):
            pair_patch(start + g, tiles, tiled, noise, force, cols, noise_t)

        repeat(stop - start, one)

    lines = size_x * size_y
    smalls[3].wait()

    def hot_patch(g):
        index = voxel[pl.ds(g, 1), :]
        hot_low[g] = one_hot(lax.rem(index, size_z), size_z)
        hot_high[g] = one_hot(lax.div(index, size_z), lines)

    repeat(patches, hot_patch, 4)

    for copy in smalls[4:]:
        copy.wait()
    early = patches // 2 + 1
    pair_range(0, early)

    for copy in flag_copies:
        copy.wait_recv()
    for copy in copies_a[2:]:
        copy.wait_recv()
    unpack_rows(post_a, row_in_a, corner_in_a)
    inside = (me_xs > 0, me_xs < n_xs - 1)
    for side in range(2):
        y = bottom if side else top
        for x in range(size_x):
            flags[x + 1, y : y + 1, :] = jnp.where(
                inside[side], row_in_a[side, 5, x : x + 1, :], 0.0
            )
    for c, k in enumerate(CORNERS):
        x, y = corner_spots(c, True)
        flags[x, y : y + 1, :] = jnp.where(
            inside[0 if LATTICE_DIRS[k][1] > 0 else 1], corner_in_a[c, 1:2, :], 0.0
        )
    repeat(size_x * blocks, bits_block, 8)

    def advance_plane(plane):
        def one_block(b):
            store_post(post_b, plane, b, collide(streamed(post_a, bits, plane, b)))

        repeat(blocks, one_block, 8)

    for plane in range(2, size_x):
        advance_plane(plane)
    copies_a[0].wait_recv()
    copies_a[1].wait_recv()
    advance_plane(size_x)
    copies_b[0].start()
    advance_plane(1)
    copies_b[1].start()
    pack_rows(post_b, row_out_b, corner_out_b)
    for copy in copies_b[2:]:
        copy.start()

    pair_range(early, patches)

    saves = [
        pltpu.make_async_copy(cells.at[:, x], pops_out.at[:, x], save_sem.at[x])
        for x in range(size_x)
    ]

    def finish_plane(plane):
        def one_block(b):
            values = streamed(post_b, bits, plane, b)
            here = block_rows(b)
            for k in range(19):
                cells[k, plane - 1, pl.ds(here, 8), :] = values[k]
            _, comps = moments(values)
            for c in range(3):
                table[plane - 1, c, pl.ds(here, 8), :] = comps[c]

        repeat(blocks, one_block, 8)
        saves[plane - 1].start()

    def gather_planes(planes, first):
        low_line, high_line = planes[0] * size_y, planes[1] * size_y
        for n, plane in enumerate(planes):
            for c in range(3):
                spot = pl.ds((2 * c + n) * size_y, size_y)
                parts[0, spot, :], parts[1, spot, :] = two_parts(table[plane, c])

        def gather_patch(g):
            line = lax.div(voxel[pl.ds(g, 1), :], size_z)
            line = jnp.where(
                line >= high_line,
                jnp.where(line < high_line + size_y, line - (high_line - size_y), -1),
                jnp.where(line < low_line + size_y, line - low_line, -1),
            )
            hit = lax.broadcasted_iota(jnp.int32, (2 * size_y, beads), 0) == line
            got = jnp.dot(parts[0], hot_low[g], preferred_element_type=F32)
            got = got + jnp.dot(parts[1], hot_low[g], preferred_element_type=F32)
            for c in range(3):
                piece = got[2 * c * size_y : 2 * (c + 1) * size_y]
                piece = VELOCITY_SCALE * jnp.where(hit, piece, 0.0).sum(axis=0, keepdims=True)
                if first:
                    flow[g, c : c + 1, :] = piece
                else:
                    flow[g, c : c + 1, :] = flow[g, c : c + 1, :] + piece

        repeat(patches, gather_patch, 8)

    for copy in copies_b[2:]:
        copy.wait_recv()
    unpack_rows(post_b, row_in_b, corner_in_b)
    finish_plane(2)
    finish_plane(3)
    gather_planes((1, 2), True)
    copies_b[0].wait_recv()
    copies_b[1].wait_recv()
    finish_plane(1)
    finish_plane(size_x)
    gather_planes((0, size_x - 1), False)
    for s in range(n_xs):
        row = jnp.int32(0)
        for g in range(patches):
            row = jnp.where(owner[g] == s, g, row)
        flow_out[s] = flow[row]
    flow_copies = to_group(flow_out, flow_in, flow_send, flow_recv)
    for copy in flow_copies:
        copy.start()
    flow_in[me_xs] = flow_out[me_xs]

    for copy in vel_copies:
        copy.wait_recv()
    def scatter_patch(g):
        reaction = -TIME_STEP * (DRAG_COEFF * (flow[g] - vel_in[owner[g]]))
        hot = hot_high[g].reshape(lines // 16, 16, beads)
        for c in range(3):
            line = jnp.broadcast_to(reaction[c : c + 1, :], (16, beads))
            for n, part in enumerate(two_parts(line)):
                scaled[n, c * lines : (c + 1) * lines, :] = (hot * part[None]).reshape(lines, beads)
        both = (((1,), (1,)), ((), ()))
        total = lax.dot_general(scaled[0], hot_low[g], both, preferred_element_type=F32)
        total = total + lax.dot_general(scaled[1], hot_low[g], both, preferred_element_type=F32)
        for c in range(3):
            field[c] = field[c] + total[c * lines : (c + 1) * lines]

    field[...] = jnp.zeros_like(field)
    repeat(patches, scatter_patch, 8)

    for copy in flow_copies:
        copy.wait_recv()
    for g in range(patches):
        drag = DRAG_COEFF * (flow_in[g] - vel_out[g])
        faster = vel_out[g] + TIME_STEP * (force[g] + drag)
        for c in range(3):
            new_vel[c, g : g + 1, :] = faster[c : c + 1, :]
    for c in range(3):
        new_pos[c] = pos[c] + TIME_STEP * new_vel[c]

    for copy in flag_copies + vel_copies + copies_a + copies_b + flow_copies:
        copy.wait_send()
    for copy in saves:
        copy.wait()


def per_device(
    n_ax, n_xs, populations, fluid_mask, patch_voxel, patch_owner, positions, velocities, pair_tiles, pair_noise
):
    size_x, size_y, size_z = fluid_mask.shape
    patches, _, beads = positions.shape
    tile = pair_noise.shape[2]
    count = beads // tile
    vmem = pl.BlockSpec(memory_space=pltpu.VMEM)
    high = size_y + 2 * PAD
    post = pltpu.VMEM((size_x + 2, 19, high, size_z), F32)
    beads3 = pltpu.VMEM((patches, 3, beads), F32)
    dma = pltpu.SemaphoreType.DMA

    def body(*refs):
        step_kernel(n_ax, n_xs, *refs)

    dist, new_pos, new_vel, field = pl.pallas_call(
        body,
        out_shape=(
            jax.ShapeDtypeStruct(populations.shape, F32),
            jax.ShapeDtypeStruct((3, patches, beads), F32),
            jax.ShapeDtypeStruct((3, patches, beads), F32),
            jax.ShapeDtypeStruct((3, size_x * size_y, size_z), F32),
        ),
        in_specs=[pl.BlockSpec(memory_space=pltpu.HBM)] * 8,
        out_specs=(pl.BlockSpec(memory_space=pl.ANY), vmem, vmem, vmem),
        scratch_shapes=[
            pltpu.SMEM((patches, 2, pair_noise.shape[1]), jnp.int32),
            pltpu.SMEM((patches,), jnp.int32),
            pltpu.VMEM((size_x, size_y, size_z), jnp.int32),
            pltpu.VMEM((patches, beads), jnp.int32),
            pltpu.VMEM((3, patches, beads), F32),
            pltpu.VMEM((3, patches, beads), F32),
            pltpu.VMEM((patches, size_z, beads), BF16),
            pltpu.VMEM((patches, size_x * size_y, beads), BF16),
            pltpu.VMEM((2, 6 * size_y, size_z), BF16),
            pltpu.VMEM(populations.shape, F32),
            post,
            post,
            pltpu.VMEM((size_x + 2, high, size_z), F32),
            pltpu.VMEM((size_x, size_y, size_z), jnp.int32),
            pltpu.VMEM(pair_noise.shape, pair_noise.dtype),
            pltpu.VMEM((2, 6, size_x, size_z), F32),
            pltpu.VMEM((2, 6, size_x, size_z), F32),
            pltpu.VMEM((4, 2, size_z), F32),
            pltpu.VMEM((4, 2, size_z), F32),
            pltpu.VMEM((2, 5, size_x, size_z), F32),
            pltpu.VMEM((2, 5, size_x, size_z), F32),
            pltpu.VMEM((4, 1, size_z), F32),
            pltpu.VMEM((4, 1, size_z), F32),
            pltpu.VMEM((2, 3 * size_x * size_y, beads), BF16),
            beads3,
            beads3,
            beads3,
            beads3,
            beads3,
            pltpu.VMEM((size_x, 3, size_y, size_z), F32),
            beads3,
            pltpu.VMEM((patches, count, 8, tile), F32),
            pltpu.VMEM((count, 6, tile, tile), F32),
            pltpu.VMEM((pair_noise.shape[1], tile, tile), F32),
            dma((size_x,)),
            dma((7,)),
            dma((size_x,)),
            dma((3, 8)),
            dma((3, 8)),
            dma((n_xs - 1,)),
            dma((n_xs - 1,)),
            dma((n_xs - 1,)),
            dma((n_xs - 1,)),
        ],
        compiler_params=pltpu.CompilerParams(
            collective_id=0, has_side_effects=True, vmem_limit_bytes=44 * 2**20
        ),
    )(
        *(
            pltpu.with_memory_space_constraint(x, pltpu.HBM)
            for x in (
                jnp.transpose(pair_tiles, (0, 2, 1)),
                patch_owner,
                populations,
                fluid_mask,
                patch_voxel,
                jnp.transpose(positions, (1, 0, 2)),
                jnp.transpose(velocities, (1, 0, 2)),
                pair_noise,
            )
        )
    )
    new_pos, new_vel = (jnp.transpose(x, (1, 0, 2)) for x in (new_pos, new_vel))
    return (dist, new_pos, new_vel, field.reshape(3, size_x, size_y, size_z))


def solution(mesh):
    n_ax, n_xs = mesh.shape["ax"], mesh.shape["xs"]

    def step(*args):
        return per_device(n_ax, n_xs, *args)

    return jax.shard_map(
        step,
        mesh=mesh,
        in_specs=(
            P(None, "ax", "xs", None),
            P("ax", "xs", None),
            P(("ax", "xs"), None),
            P(("ax", "xs")),
            P(("ax", "xs"), None, None),
            P(("ax", "xs"), None, None),
            P(("ax", "xs"), None, None),
            P(("ax", "xs"), None, None, None),
        ),
        out_specs=(
            P(None, "ax", "xs", None),
            P(("ax", "xs"), None, None),
            P(("ax", "xs"), None, None),
            P(None, "ax", "xs", None),
        ),
        check_vma=False,
    )
```
